512 devices in a mesh: batch: 16 (over y, core), seq: 32 (over x, z).
Axes of the slice: x: 4, y: 8, z: 8, core: 2. Of those that a mesh axis runs over, the one named last changes fastest.
Arguments:
- values: bfloat16 [1024, 131072], P(None, ('batch', 'seq')), may hold values from -6 to 6
- gates: bfloat16 [1024, 131072], P(None, ('batch', 'seq')), may hold values from -6 to 6
- cotangent: bfloat16 [1024, 131072], P(None, ('batch', 'seq')), may hold values from -12 to 12
- taps_values: float32 [3, 1024], replicated, may hold values from -3 to 3
- taps_gates: float32 [3, 1024], replicated, may hold values from -3 to 3
- skip_gain: float32 [1024], replicated, may hold values from 0.5 to 1.5
- twiddle: float32 [128, 1024], P('batch'), may hold values from 0.5 to 1.5
- mixing: float32 [128, 128], replicated, may hold values from -2 to 3
- spectrum: bfloat16 [1024, 128, 1024], P('seq', None, 'batch'), may hold values from -4 to 4
Outputs:
- mixed: bfloat16 [1024, 131072], P(None, ('batch', 'seq'))
- grad_values: bfloat16 [1024, 131072], P(None, ('batch', 'seq'))
- grad_gates: bfloat16 [1024, 131072], P(None, ('batch', 'seq'))
- grad_spectrum: float32 [1024, 128, 1024], P('seq', None, 'batch')
- grad_taps_values: float32 [3, 1024], P(None, 'seq')
- grad_taps_gates: float32 [3, 1024], P(None, 'seq')
- grad_skip: float32 [1024], P('seq')
The draws below stay inside these ranges and needn't reach their ends.
All inputs are finite; a program needn't handle non-finite values.
Results may differ from the reference program's by a relative error of at most 0.0085.
Values may be sent and summed in bfloat16 or wider, within the bound.
No kernel may reach another device: no remote copies, remote signals or barrier semaphores. Data moves between devices by JAX's collectives and lax.ppermute only.
A program may use at most 64 MiB of HBM per device.

```python
import math
import jax
import jax.numpy as jnp
from jax import lax

D = 1024
BLOCK = 1024
LENGTH = 131072
BLOCKS = 128


def draw_cotangent(key, part):
    first_key = jax.random.fold_in(key, 0)
    base = jax.random.truncated_normal(first_key, -6.0, 6.0, (D, LENGTH), jnp.float32)
    along = 1.0 + 2.0 * jnp.arange(LENGTH, dtype=jnp.float32) / max(LENGTH - 1, 1)
    result = 0.5 * base * along[None, :]
    return result.astype(jnp.bfloat16)


def draw_mixing(key, part):
    positions = jnp.arange(BLOCKS, dtype=jnp.int32)
    diagonal = (positions[:, None] == positions[None, :]).astype(jnp.float32)
    noise = jax.random.truncated_normal(key, -3.0, 3.0, (BLOCKS, BLOCKS), jnp.float32)
    return diagonal + 0.6 / BLOCKS ** 0.5 * noise


def block_scale(own_key, shape, pieces, smallest, high):
    def one(axis_at, parts):
        steps = jax.random.uniform(jax.random.fold_in(jax.random.fold_in(own_key, 6), axis_at), (parts,), jnp.float32, smallest / len(pieces), high / len(pieces))
        return jnp.repeat(jnp.exp(steps), shape[axis_at] // parts).reshape((-1,) + (1,) * (len(shape) - axis_at - 1))

    factor_of = one(*pieces[0])
    for cut in pieces[1:]:
        factor_of = factor_of * one(*cut)
    return factor_of


def scatter_about(key, extent, scale, bound, shards=(), kind=jnp.bfloat16):
    values = jax.random.normal(key, extent, jnp.float32) * scale
    if len(shards) > 0:
        values = block_scale(key, extent, shards, -0.22, 0.18) * values
    return jnp.clip(values, min=-bound, max=bound).astype(kind)


def setup_inputs(seed: int = 0) -> dict:
    arg_keys = jax.random.split(jax.random.key(seed), 10)
    return {
        "values": scatter_about(arg_keys[0], (D, LENGTH), 1.0, 6.0, ((1, 512),)),
        "gates": scatter_about(arg_keys[1], (D, LENGTH), 1.0, 6.0, ((1, 512),)),
        "cotangent": draw_cotangent(jax.random.fold_in(arg_keys[9], 71), 0),
        "taps_values": scatter_about(arg_keys[3], (3, D), 0.6, 3.0, (), jnp.float32),
        "taps_gates": scatter_about(arg_keys[4], (3, D), 0.6, 3.0, (), jnp.float32),
        "skip_gain": jnp.clip(jax.random.uniform(arg_keys[5], (D,), jnp.float32, 0.5, 1.5), 0.5, 1.5),
        "twiddle": jnp.clip(0.5 + 1.0 * jax.random.uniform(arg_keys[6], (BLOCKS, BLOCK), jnp.float32) ** block_scale(arg_keys[6], (BLOCKS, BLOCK), ((0, 16),), -0.2, 0.2), 0.5, 1.5),
        "mixing": draw_mixing(jax.random.fold_in(arg_keys[9], 71), 0),
        "spectrum": scatter_about(arg_keys[8], (D, BLOCKS, BLOCK), 1.0, 4.0, ((0, 32), (2, 16))),
    }


def cas_table():
    indices = jnp.arange(BLOCK, dtype=jnp.int32)
    products = indices[:, None] * indices[None, :] % BLOCK
    angles = products.astype(jnp.float32) * (2.0 * math.pi / BLOCK)
    return ((jnp.cos(angles) + jnp.sin(angles)) / math.sqrt(BLOCK)).astype(jnp.bfloat16)

def transform(source, cas_matrix, twiddle, mixing):
    channels = source.shape[0]
    block_sums = jnp.dot(source.reshape(-1, BLOCK), cas_matrix, preferred_element_type=jnp.float32)
    block_sums = block_sums.reshape(channels, -1, BLOCK) * twiddle
    return jnp.einsum('pi,cik->cpk', mixing, block_sums, precision=lax.Precision.HIGHEST)

def back(spectra, cas_matrix, twiddle, mixing):
    channels = spectra.shape[0]
    weighted = jnp.einsum('ip,cik->cpk', mixing, spectra, precision=lax.Precision.HIGHEST) * twiddle
    weighted = weighted.astype(jnp.bfloat16)
    result = jnp.dot(weighted.reshape(-1, BLOCK), cas_matrix, preferred_element_type=jnp.float32)
    return result.reshape(channels, -1).astype(jnp.bfloat16)

def reference(values, gates, cotangent, taps_values, taps_gates, skip_gain, twiddle, mixing, spectrum):
    cas_matrix = cas_table()
    group_size = math.gcd(D, 64)
    group_count = D // group_size

    def split_rows(array):
        return array.reshape(group_count, group_size, LENGTH)

    def split_taps(taps):
        return taps.reshape(3, group_count, group_size).transpose(1, 0, 2)

    def one_group(inputs):
        value_rows, gate_rows, cot_rows, value_taps, gate_taps, skip_part, filter_part = inputs
        filters = filter_part.astype(jnp.float32)
        skip_col = skip_part[:, None]
        wide_values = jnp.pad(value_rows.astype(jnp.float32), ((0, 0), (2, 0)))
        wide_gates = jnp.pad(gate_rows.astype(jnp.float32), ((0, 0), (2, 0)))
        short_values = (value_taps[0][:, None] * wide_values[:, 2:] + value_taps[1][:, None] * wide_values[:, 1:-1] + value_taps[2][:, None] * wide_values[:, :-2]).astype(jnp.bfloat16)
        short_gates = gate_taps[0][:, None] * wide_gates[:, 2:] + gate_taps[1][:, None] * wide_gates[:, 1:-1] + gate_taps[2][:, None] * wide_gates[:, :-2]
        cotangent_f32 = cot_rows.astype(jnp.float32)
        grad_long = (cotangent_f32 * short_gates).astype(jnp.bfloat16)
        spectra_values = transform(short_values, cas_matrix, twiddle, mixing)
        long_values = back(spectra_values * filters, cas_matrix, twiddle, mixing)
        spectra_grads = transform(grad_long, cas_matrix, twiddle, mixing)
        back_grads = back(spectra_grads * filters, cas_matrix, twiddle, mixing)
        long_f32 = long_values.astype(jnp.float32)
        short_f32 = short_values.astype(jnp.float32)
        mixed = (short_gates * (long_f32 + skip_col * short_f32)).astype(jnp.bfloat16)
        grad_short_gates = cotangent_f32 * (long_f32 + skip_col * short_f32)
        long_grad_f32 = grad_long.astype(jnp.float32)
        grad_short_values = skip_col * long_grad_f32 + back_grads.astype(jnp.float32)
        ahead_values = jnp.pad(grad_short_values, ((0, 0), (0, 2)))
        ahead_gates = jnp.pad(grad_short_gates, ((0, 0), (0, 2)))
        grad_values = (value_taps[0][:, None] * ahead_values[:, :-2] + value_taps[1][:, None] * ahead_values[:, 1:-1] + value_taps[2][:, None] * ahead_values[:, 2:]).astype(jnp.bfloat16)
        grad_gates = (gate_taps[0][:, None] * ahead_gates[:, :-2] + gate_taps[1][:, None] * ahead_gates[:, 1:-1] + gate_taps[2][:, None] * ahead_gates[:, 2:]).astype(jnp.bfloat16)
        local_taps_values = jnp.stack([lax.optimization_barrier(jnp.sum(grad_short_values * wide_values[:, 2:], axis=1)), lax.optimization_barrier(jnp.sum(grad_short_values * wide_values[:, 1:-1], axis=1)), lax.optimization_barrier(jnp.sum(grad_short_values * wide_values[:, :-2], axis=1))], axis=0)
        local_taps_gates = jnp.stack([lax.optimization_barrier(jnp.sum(grad_short_gates * wide_gates[:, 2:], axis=1)), lax.optimization_barrier(jnp.sum(grad_short_gates * wide_gates[:, 1:-1], axis=1)), lax.optimization_barrier(jnp.sum(grad_short_gates * wide_gates[:, :-2], axis=1))], axis=0)
        local_skip = lax.optimization_barrier(jnp.sum(long_grad_f32 * short_f32, axis=1))
        grad_spectrum = spectra_values * spectra_grads
        return (mixed, grad_values, grad_gates, grad_spectrum, local_taps_values, local_taps_gates, local_skip)
    inputs = (split_rows(values), split_rows(gates), split_rows(cotangent), split_taps(taps_values), split_taps(taps_gates), skip_gain.reshape(group_count, group_size), spectrum.reshape(group_count, group_size, BLOCKS, BLOCK))
    results = lax.map(one_group, inputs)
    mixed = results[0].reshape(D, LENGTH)
    grad_values = results[1].reshape(D, LENGTH)
    grad_gates = results[2].reshape(D, LENGTH)
    grad_spectrum = results[3].reshape(D, BLOCKS, BLOCK)
    grad_taps_values = results[4].transpose(1, 0, 2).reshape(3, D)
    grad_taps_gates = results[5].transpose(1, 0, 2).reshape(3, D)
    grad_skip = results[6].reshape(D)
    return (mixed, grad_values, grad_gates, grad_spectrum, grad_taps_values, grad_taps_gates, grad_skip)
```

```python
import functools
import math

import jax
import jax.numpy as jnp
import numpy as np
from jax import lax
from jax.experimental import pallas as pl
from jax.experimental.pallas import tpu as pltpu
from jax.sharding import PartitionSpec as P

BLOCK = 1024
F32, BF16 = jnp.float32, jnp.bfloat16


def cas_table():
    indices = np.arange(BLOCK, dtype=np.int32)
    products = indices[:, None] * indices[None, :] % BLOCK
    angles = products.astype(np.float32) * np.float32(2.0 * math.pi / BLOCK)
    table = (np.cos(angles) + np.sin(angles)) / np.float32(math.sqrt(BLOCK))
    return table.astype(jnp.bfloat16)


def lanes(shape=(32, 128)):
    return lax.broadcasted_iota(jnp.int32, shape, 1)


def back_in_time(now, before, steps, lane):
    return jnp.where(lane < steps, before, now)


def rolled(tile):
    return pltpu.roll(tile, 1, 1), pltpu.roll(tile, 2, 1)


def column(cols, at):
    return jnp.broadcast_to(cols[:, at : at + 1], (32, 128))


def spread_kernel(r_ref, rim_ref, cols_ref, tw_ref, cas_ref, out_ref, lhs):
    lane = lanes()
    cols = cols_ref[...]
    tv = [column(cols, k) for k in range(3)]
    tg = [column(cols, 3 + k) for k in range(3)]

    def block(i, carry):
        v1, v2, g1, g2 = carry
        rows = pl.multiple_of(i * 32, 32)
        for t in range(8):
            piece, at = i * 4 + t // 2, (t % 2) * 128
            v = r_ref[piece, 0:32, at : at + 128].astype(F32)
            g = r_ref[piece, 32:64, at : at + 128].astype(F32)
            c = r_ref[piece, 64:96, at : at + 128].astype(F32)
            nv1, nv2 = rolled(v)
            ng1, ng2 = rolled(g)
            short_v = tv[0] * v + tv[1] * back_in_time(nv1, v1, 1, lane) + tv[2] * back_in_time(nv2, v2, 2, lane)
            short_g = tg[0] * g + tg[1] * back_in_time(ng1, g1, 1, lane) + tg[2] * back_in_time(ng2, g2, 2, lane)
            lhs[pl.ds(rows, 32), t * 128 : t * 128 + 128] = short_v.astype(BF16)
            lhs[pl.ds(rows + 256, 32), t * 128 : t * 128 + 128] = (c * short_g).astype(BF16)
            v1, v2, g1, g2 = nv1, nv2, ng1, ng2
        return v1, v2, g1, g2

    start = rolled(rim_ref[0:32, :].astype(F32)) + rolled(rim_ref[32:64, :].astype(F32))
    lax.fori_loop(0, 8, block, start)

    low = lanes((16, 128)) < 64

    def strip(n, _):
        at = pl.multiple_of(n * 256, 256)
        sums = jnp.dot(lhs[...], cas_ref[:, pl.ds(at, 256)], preferred_element_type=F32)
        for h in range(2):
            tw = tw_ref[:, pl.ds(pl.multiple_of(at + h * 128, 128), 128)]
            d = 4 * n + 2 * h
            for m in range(16):
                part = sums[m * 32 : m * 32 + 32, h * 128 : h * 128 + 128] * tw[m % 8 : m % 8 + 1, :]
                a, b = part[:16], part[16:]
                even = jnp.where(low, a, pltpu.roll(b, 64, 1))
                odd = jnp.where(low, pltpu.roll(a, 64, 1), b)
                out_ref[d, m * 16 : m * 16 + 16, :] = even.astype(BF16)
                out_ref[d + 1, m * 16 : m * 16 + 16, :] = odd.astype(BF16)
        return 0

    lax.fori_loop(0, 4, strip, 0)


def mix_kernel(f_ref, spec_ref, mix_ref, gs_ref, out_ref, wide_v, wide_g):
    wide = (wide_v, wide_g)
    for f in range(2):
        for b in range(16):
            wide[f][b * 128 : b * 128 + 128, :] = f_ref[b, f * 128 : f * 128 + 128, :].astype(F32)
    mixing = mix_ref[...]
    turned = mixing.T
    high = turned.astype(BF16)
    low = (turned - high.astype(F32)).astype(BF16)
    ahead = jnp.concatenate([high, low], axis=1)
    again = jnp.concatenate([jnp.concatenate([high, high], axis=1), jnp.concatenate([low, low], axis=1)], axis=0)

    for c in range(16):
        slabs = [wide[f][pl.ds(c, 128, stride=16), :].T.astype(BF16) for f in range(2)]
        both = jnp.dot(jnp.concatenate(slabs, axis=0), ahead, preferred_element_type=F32)
        both = both[:, :128] + both[:, 128:]
        sv, sg = both[:128], both[128:]
        filters = jnp.concatenate([spec_ref[c], spec_ref[16 + c]], axis=0).astype(F32)
        grad = sv * sg
        gs_ref[c] = grad[:64]
        gs_ref[16 + c] = grad[64:]
        product = jnp.concatenate([sv * filters, sg * filters], axis=0)
        top = product.astype(BF16)
        rest = (product - top.astype(F32)).astype(BF16)
        product = jnp.concatenate([top, rest], axis=1)
        sums = lax.dot_general(again, product, (((1,), (1,)), ((), ())), preferred_element_type=F32)
        sums = sums[:128] + sums[128:]
        for f in range(2):
            wide[f][pl.ds(c, 128, stride=16), :] = sums[:, f * 128 : f * 128 + 128]
    for f in range(2):
        for b in range(16):
            out_ref[b, f * 128 : f * 128 + 128, :] = wide[f][b * 128 : b * 128 + 128, :].astype(BF16)


def back_kernel(y_ref, r_ref, rim_ref, cols_ref, tw_ref, cas_ref, out_ref, head_ref, lhs):
    low = lanes((16, 128)) < 64

    def unpack(y, _):
        at = pl.multiple_of(y * 128, 128)
        tw = tw_ref[:, pl.ds(at, 128)]
        for m in range(16):
            e = y_ref[2 * y, m * 16 : m * 16 + 16, :].astype(F32)
            o = y_ref[2 * y + 1, m * 16 : m * 16 + 16, :].astype(F32)
            row = tw[m % 8 : m % 8 + 1, :]
            a = jnp.where(low, e, pltpu.roll(o, 64, 1)) * row
            b = jnp.where(low, pltpu.roll(e, 64, 1), o) * row
            lhs[m * 32 : m * 32 + 16, pl.ds(at, 128)] = a.astype(BF16)
            lhs[m * 32 + 16 : m * 32 + 32, pl.ds(at, 128)] = b.astype(BF16)
        return 0

    lax.fori_loop(0, 8, unpack, 0)

    def strip(n, _):
        at = pl.multiple_of(n * 256, 256)
        sums = jnp.dot(lhs[...], cas_ref[:, pl.ds(at, 256)], preferred_element_type=F32)
        out_ref[:, pl.ds(at, 256)] = sums.astype(BF16)
        return 0

    lax.fori_loop(0, 4, strip, 0)

    lane = lanes()
    cols = cols_ref[...]
    v, g, c = (r_ref[0, k * 32 : k * 32 + 32, 0:128].astype(F32) for k in range(3))
    before_v, before_g = rim_ref[0:32, :].astype(F32), rim_ref[32:64, :].astype(F32)
    short_v, short_g = v * column(cols, 0), g * column(cols, 3)
    for k in (1, 2):
        short_v += column(cols, k) * back_in_time(pltpu.roll(v, k, 1), pltpu.roll(before_v, k, 1), k, lane)
        short_g += column(cols, 3 + k) * back_in_time(pltpu.roll(g, k, 1), pltpu.roll(before_g, k, 1), k, lane)
    short_v = short_v.astype(BF16).astype(F32)
    grad_long = (c * short_g).astype(BF16).astype(F32)
    skip = column(cols, 6)
    head_ref[0:32, :] = skip * grad_long + out_ref[256:288, 0:128].astype(F32)
    head_ref[32:64, :] = c * (out_ref[0:32, 0:128].astype(F32) + skip * short_v)


def final_kernel(d_ref, r_ref, rim_ref, next_ref, cols_ref, out_ref, sums_ref):
    lane = lanes()
    cols = cols_ref[...]
    tv = [column(cols, k) for k in range(3)]
    tg = [column(cols, 3 + k) for k in range(3)]
    skip = column(cols, 6)

    def ahead(tile):
        return pltpu.roll(tile, 127, 1), pltpu.roll(tile, 126, 1)

    def block(step, carry):
        i = 7 - step
        (v, v1, v2), (g, g1, g2), nv, ng, acc = carry
        rows = pl.multiple_of(i * 32, 32)
        for t in reversed(range(8)):
            piece, at = i * 4 + t // 2, (t % 2) * 128
            if t > 0:
                piece_b, at_b = i * 4 + (t - 1) // 2, ((t - 1) % 2) * 128
                pv = r_ref[piece_b, 0:32, at_b : at_b + 128].astype(F32)
                pg = r_ref[piece_b, 32:64, at_b : at_b + 128].astype(F32)
            else:
                inside = i > 0
                piece_b = jnp.maximum(i * 4 - 1, 0)
                pv = jnp.where(inside, r_ref[piece_b, 0:32, 128:256].astype(F32), rim_ref[0:32, :].astype(F32))
                pg = jnp.where(inside, r_ref[piece_b, 32:64, 128:256].astype(F32), rim_ref[32:64, :].astype(F32))
            pv1, pv2 = rolled(pv)
            pg1, pg2 = rolled(pg)
            vb1, vb2 = back_in_time(v1, pv1, 1, lane), back_in_time(v2, pv2, 2, lane)
            gb1, gb2 = back_in_time(g1, pg1, 1, lane), back_in_time(g2, pg2, 2, lane)
            short_v = (tv[0] * v + tv[1] * vb1 + tv[2] * vb2).astype(BF16).astype(F32)
            short_g = tg[0] * g + tg[1] * gb1 + tg[2] * gb2
            c = r_ref[piece, 64:96, at : at + 128].astype(F32)
            grad_long = (c * short_g).astype(BF16).astype(F32)
            long_v = d_ref[pl.ds(rows, 32), t * 128 : t * 128 + 128].astype(F32)
            back_g = d_ref[pl.ds(rows + 256, 32), t * 128 : t * 128 + 128].astype(F32)
            direct = long_v + skip * short_v
            gsg = c * direct
            gsv = skip * grad_long + back_g
            wv, wg = ahead(gsv), ahead(gsg)
            out_ref[piece, 0:32, at : at + 128] = (short_g * direct).astype(BF16)
            out_ref[piece, 32:64, at : at + 128] = (
                tv[0] * gsv + tv[1] * jnp.where(lane > 126, nv[0], wv[0]) + tv[2] * jnp.where(lane > 125, nv[1], wv[1])
            ).astype(BF16)
            out_ref[piece, 64:96, at : at + 128] = (
                tg[0] * gsg + tg[1] * jnp.where(lane > 126, ng[0], wg[0]) + tg[2] * jnp.where(lane > 125, ng[1], wg[1])
            ).astype(BF16)
            terms = (gsv * v, gsv * vb1, gsv * vb2, gsg * g, gsg * gb1, gsg * gb2, grad_long * short_v)
            acc = tuple(a + b for a, b in zip(acc, terms))
            v, v1, v2, g, g1, g2, nv, ng = pv, pv1, pv2, pg, pg1, pg2, wv, wg
        return (v, v1, v2), (g, g1, g2), nv, ng, acc

    last_v = r_ref[31, 0:32, 128:256].astype(F32)
    last_g = r_ref[31, 32:64, 128:256].astype(F32)
    zero = jnp.zeros((32, 128), F32)
    start = (
        (last_v, *rolled(last_v)),
        (last_g, *rolled(last_g)),
        ahead(next_ref[0:32, :]),
        ahead(next_ref[32:64, :]),
        (zero,) * 7,
    )
    acc = lax.fori_loop(0, 8, block, start)[4]
    total = zero
    for k in range(7):
        total = jnp.where(lane == k, jnp.sum(acc[k], axis=1, keepdims=True), total)
    sums_ref[...] = total


def call(kernel, outs, scratch, flops, moved, *args):
    return pl.pallas_call(
        kernel,
        out_shape=[jax.ShapeDtypeStruct(s, d) for s, d in outs],
        scratch_shapes=[pltpu.VMEM(s, d) for s, d in scratch],
        cost_estimate=pl.CostEstimate(flops=flops, bytes_accessed=moved, transcendentals=0),
    )(*args)


def spread(r, rim, cols, twiddle, cas):
    return call(spread_kernel, [((16, 256, 128), BF16)], [((512, 1024), BF16)], 1 << 30, 5 << 20, r, rim, cols, twiddle, cas)[0]


def mix(by_freq, spectrum, mixing):
    return call(
        mix_kernel,
        [((32, 64, 128), F32), ((16, 256, 128), BF16)],
        [((2048, 128), F32), ((2048, 128), F32)],
        1 << 30,
        5 << 20,
        by_freq,
        spectrum,
        mixing,
    )


def back(returned, r, rim, cols, twiddle, cas):
    return call(
        back_kernel,
        [((512, 1024), BF16), ((64, 128), F32)],
        [((512, 1024), BF16)],
        1 << 30,
        5 << 20,
        returned,
        r,
        rim,
        cols,
        twiddle,
        cas,
    )


def final(d, r, rim, following, cols):
    return call(
        final_kernel, [((32, 96, 256), BF16), ((32, 128), F32)], [], 1 << 24, 5 << 20, d, r, rim, following, cols
    )


def exchange(array, axis):
    return lax.all_to_all(array, axis, 0, 0, tiled=True)


def per_device(values, gates, cotangent, taps_values, taps_gates, skip_gain, twiddle, mixing, spectrum):
    batch = lax.axis_size("batch")
    cas = jnp.asarray(cas_table())
    raw = jnp.concatenate([x.reshape(32, 32, 256) for x in (values, gates, cotangent)], axis=1)
    r = exchange(raw, "seq")
    gains = jnp.concatenate([taps_values, taps_gates, skip_gain[None]], axis=0)
    cols = lax.dynamic_slice(gains, (0, lax.axis_index("seq") * 32), (7, 32))
    cols = jnp.pad(cols.T, ((0, 0), (0, 121)))
    rim = lax.ppermute(r[31, :64, 128:], "batch", [(i, i + 1) for i in range(batch - 1)])
    by_freq = exchange(spread(r, rim, cols, twiddle, cas), "batch")
    grad_spectrum, weighted = mix(by_freq, spectrum.transpose(0, 2, 1), mixing)
    d, head = back(exchange(weighted, "batch"), r, rim, cols, twiddle, cas)
    following = lax.ppermute(head, "batch", [(i + 1, i) for i in range(batch - 1)])
    done, sums = final(d, r, rim, following, cols)
    outs = exchange(done, "seq")
    step = 1
    while step < batch:
        sums = sums + lax.ppermute(sums, "batch", [(i, i ^ step) for i in range(batch)])
        step *= 2
    sums = sums[:, :7].T
    mixed, grad_values, grad_gates = (outs[:, k * 32 : k * 32 + 32].reshape(values.shape) for k in range(3))
    return mixed, grad_values, grad_gates, grad_spectrum.transpose(0, 2, 1), sums[0:3], sums[3:6], sums[6]


def solution(mesh):
    in_specs = (
        P(None, ("batch", "seq")),
        P(None, ("batch", "seq")),
        P(None, ("batch", "seq")),
        P(),
        P(),
        P(),
        P("batch", None),
        P(),
        P("seq", None, "batch"),
    )
    out_specs = (
        P(None, ("batch", "seq")),
        P(None, ("batch", "seq")),
        P(None, ("batch", "seq")),
        P("seq", None, "batch"),
        P(None, "seq"),
        P(None, "seq"),
        P("seq"),
    )
    return jax.shard_map(per_device, mesh=mesh, in_specs=in_specs, out_specs=out_specs, check_vma=False)
```

```python
import functools
import math

import jax
import jax.numpy as jnp
import numpy as np
from jax import lax
from jax.experimental import pallas as pl
from jax.experimental.pallas import tpu as pltpu
from jax.sharding import PartitionSpec as P

BLOCK = 1024
F32, BF16 = jnp.float32, jnp.bfloat16
GRANT = 20 << 20


def cas_table():
    indices = np.arange(BLOCK, dtype=np.int32)
    products = indices[:, None] * indices[None, :] % BLOCK
    angles = products.astype(np.float32) * np.float32(2.0 * math.pi / BLOCK)
    table = (np.cos(angles) + np.sin(angles)) / np.float32(math.sqrt(BLOCK))
    return table.astype(jnp.bfloat16)


def lanes(shape=(32, 128)):
    return lax.broadcasted_iota(jnp.int32, shape, 1)


def back_in_time(now, before, steps, lane):
    return jnp.where(lane < steps, before, now)


def rolled(tile):
    return pltpu.roll(tile, 1, 1), pltpu.roll(tile, 2, 1)


def column(cols, at):
    return jnp.broadcast_to(cols[:, at : at + 1], (cols.shape[0], 128))


def gather_kernel(a_ref, b_ref, c_ref, out_ref, sems):
    copies = [
        pltpu.make_async_copy(ref, out_ref.at[:, k * 32 : k * 32 + 32, :], sems.at[k])
        for k, ref in enumerate((a_ref, b_ref, c_ref))
    ]
    for copy in copies:
        copy.start()
    for copy in copies:
        copy.wait()


def spread_kernel(r_ref, rim_ref, cols_ref, tw_ref, cas_ref, out_ref, lhs):
    lane = lanes((16, 128))
    for h in range(2):
        own = slice(h * 16, h * 16 + 16)
        cols = cols_ref[own, :]
        tv = [column(cols, k) for k in range(3)]
        tg = [column(cols, 3 + k) for k in range(3)]

        def block(i, carry):
            v1, v2, g1, g2 = carry
            rows = pl.multiple_of(i * 32, 32) + h * 16
            for t in range(8):
                piece, at = i * 4 + t // 2, slice((t % 2) * 128, (t % 2) * 128 + 128)
                v = r_ref[piece, own, at].astype(F32)
                g = r_ref[piece, h * 16 + 32 : h * 16 + 48, at].astype(F32)
                c = r_ref[piece, h * 16 + 64 : h * 16 + 80, at].astype(F32)
                nv1, nv2 = rolled(v)
                ng1, ng2 = rolled(g)
                short_v = tv[0] * v + tv[1] * back_in_time(nv1, v1, 1, lane) + tv[2] * back_in_time(nv2, v2, 2, lane)
                short_g = tg[0] * g + tg[1] * back_in_time(ng1, g1, 1, lane) + tg[2] * back_in_time(ng2, g2, 2, lane)
                lhs[pl.ds(rows, 16), t * 128 : t * 128 + 128] = short_v.astype(BF16)
                lhs[pl.ds(rows + 256, 16), t * 128 : t * 128 + 128] = (c * short_g).astype(BF16)
                v1, v2, g1, g2 = nv1, nv2, ng1, ng2
            return v1, v2, g1, g2

        start = rolled(rim_ref[own, :].astype(F32)) + rolled(rim_ref[h * 16 + 32 : h * 16 + 48, :].astype(F32))
        lax.fori_loop(0, 8, block, start)

    low = lanes((16, 128)) < 64

    def strip(n, _):
        at = pl.multiple_of(n * 256, 256)
        sums = jnp.dot(lhs[...], cas_ref[:, pl.ds(at, 256)], preferred_element_type=F32)
        for h in range(2):
            tw = tw_ref[:, pl.ds(pl.multiple_of(at + h * 128, 128), 128)]
            d = 4 * n + 2 * h
            for m in range(16):
                part = sums[m * 32 : m * 32 + 32, h * 128 : h * 128 + 128] * tw[m % 8 : m % 8 + 1, :]
                a, b = part[:16], part[16:]
                even = jnp.where(low, a, pltpu.roll(b, 64, 1))
                odd = jnp.where(low, pltpu.roll(a, 64, 1), b)
                out_ref[d, m * 16 : m * 16 + 16, :] = even.astype(BF16)
                out_ref[d + 1, m * 16 : m * 16 + 16, :] = odd.astype(BF16)
        return 0

    lax.fori_loop(0, 4, strip, 0)


def mix_kernel(f_ref, spec_ref, mix_ref, gs_ref, out_ref, wide_v, wide_g):
    wide = (wide_v, wide_g)
    for f in range(2):
        for b in range(16):
            wide[f][b * 128 : b * 128 + 128, :] = f_ref[b, f * 128 : f * 128 + 128, :].astype(F32)
    mixing = mix_ref[...]
    turned = mixing.T
    high = turned.astype(BF16)
    low = (turned - high.astype(F32)).astype(BF16)
    ahead = jnp.concatenate([high, low], axis=1)
    again = jnp.concatenate([jnp.concatenate([high, high], axis=1), jnp.concatenate([low, low], axis=1)], axis=0)

    for c in range(16):
        slabs = [wide[f][pl.ds(c, 128, stride=16), :].T.astype(BF16) for f in range(2)]
        both = jnp.dot(jnp.concatenate(slabs, axis=0), ahead, preferred_element_type=F32)
        both = both[:, :128] + both[:, 128:]
        sv, sg = both[:128], both[128:]
        filters = jnp.concatenate([spec_ref[c], spec_ref[16 + c]], axis=0).astype(F32)
        grad = sv * sg
        gs_ref[c] = grad[:64]
        gs_ref[16 + c] = grad[64:]
        product = jnp.concatenate([sv * filters, sg * filters], axis=0)
        top = product.astype(BF16)
        rest = (product - top.astype(F32)).astype(BF16)
        product = jnp.concatenate([top, rest], axis=1)
        sums = lax.dot_general(again, product, (((1,), (1,)), ((), ())), preferred_element_type=F32)
        sums = sums[:128] + sums[128:]
        for f in range(2):
            wide[f][pl.ds(c, 128, stride=16), :] = sums[:, f * 128 : f * 128 + 128]
    for f in range(2):
        for b in range(16):
            out_ref[b, f * 128 : f * 128 + 128, :] = wide[f][b * 128 : b * 128 + 128, :].astype(BF16)


def back_kernel(y_ref, r_ref, rim_ref, cols_ref, tw_ref, cas_ref, out_ref, head_ref, lhs):
    low = lanes((16, 128)) < 64

    def unpack(y, _):
        at = pl.multiple_of(y * 128, 128)
        tw = tw_ref[:, pl.ds(at, 128)]
        for m in range(16):
            e = y_ref[2 * y, m * 16 : m * 16 + 16, :].astype(F32)
            o = y_ref[2 * y + 1, m * 16 : m * 16 + 16, :].astype(F32)
            row = tw[m % 8 : m % 8 + 1, :]
            a = jnp.where(low, e, pltpu.roll(o, 64, 1)) * row
            b = jnp.where(low, pltpu.roll(e, 64, 1), o) * row
            lhs[m * 32 : m * 32 + 16, pl.ds(at, 128)] = a.astype(BF16)
            lhs[m * 32 + 16 : m * 32 + 32, pl.ds(at, 128)] = b.astype(BF16)
        return 0

    lax.fori_loop(0, 8, unpack, 0)

    def strip(n, _):
        at = pl.multiple_of(n * 256, 256)
        sums = jnp.dot(lhs[...], cas_ref[:, pl.ds(at, 256)], preferred_element_type=F32)
        out_ref[:, pl.ds(at, 256)] = sums.astype(BF16)
        return 0

    lax.fori_loop(0, 4, strip, 0)

    lane = lanes()
    cols = cols_ref[...]
    v, g, c = (r_ref[0, k * 32 : k * 32 + 32, 0:128].astype(F32) for k in range(3))
    before_v, before_g = rim_ref[0:32, :].astype(F32), rim_ref[32:64, :].astype(F32)
    short_v, short_g = v * column(cols, 0), g * column(cols, 3)
    for k in (1, 2):
        short_v += column(cols, k) * back_in_time(pltpu.roll(v, k, 1), pltpu.roll(before_v, k, 1), k, lane)
        short_g += column(cols, 3 + k) * back_in_time(pltpu.roll(g, k, 1), pltpu.roll(before_g, k, 1), k, lane)
    short_v = short_v.astype(BF16).astype(F32)
    grad_long = (c * short_g).astype(BF16).astype(F32)
    skip = column(cols, 6)
    head_ref[0:32, :] = skip * grad_long + out_ref[256:288, 0:128].astype(F32)
    head_ref[32:64, :] = c * (out_ref[0:32, 0:128].astype(F32) + skip * short_v)


def final_kernel(d_ref, r_ref, rim_ref, next_ref, cols_ref, out_ref, sums_ref):
    lane = lanes((16, 128))

    def ahead(tile):
        return pltpu.roll(tile, 127, 1), pltpu.roll(tile, 126, 1)

    for h in range(2):
        one, two, three = (slice(h * 16 + k * 32, h * 16 + k * 32 + 16) for k in range(3))
        cols = cols_ref[one, :]
        tv = [column(cols, k) for k in range(3)]
        tg = [column(cols, 3 + k) for k in range(3)]
        skip = column(cols, 6)

        def block(step, carry):
            i = 7 - step
            (v, v1, v2), (g, g1, g2), nv, ng, acc = carry
            rows = pl.multiple_of(i * 32, 32) + h * 16
            for t in reversed(range(8)):
                piece, at = i * 4 + t // 2, slice((t % 2) * 128, (t % 2) * 128 + 128)
                if t > 0:
                    piece_b, at_b = i * 4 + (t - 1) // 2, slice(((t - 1) % 2) * 128, ((t - 1) % 2) * 128 + 128)
                    pv = r_ref[piece_b, one, at_b].astype(F32)
                    pg = r_ref[piece_b, two, at_b].astype(F32)
                else:
                    inside = i > 0
                    piece_b = jnp.maximum(i * 4 - 1, 0)
                    pv = jnp.where(inside, r_ref[piece_b, one, 128:256].astype(F32), rim_ref[one, :].astype(F32))
                    pg = jnp.where(inside, r_ref[piece_b, two, 128:256].astype(F32), rim_ref[two, :].astype(F32))
                pv1, pv2 = rolled(pv)
                pg1, pg2 = rolled(pg)
                vb1, vb2 = back_in_time(v1, pv1, 1, lane), back_in_time(v2, pv2, 2, lane)
                gb1, gb2 = back_in_time(g1, pg1, 1, lane), back_in_time(g2, pg2, 2, lane)
                short_v = (tv[0] * v + tv[1] * vb1 + tv[2] * vb2).astype(BF16).astype(F32)
                short_g = tg[0] * g + tg[1] * gb1 + tg[2] * gb2
                c = r_ref[piece, three, at].astype(F32)
                grad_long = (c * short_g).astype(BF16).astype(F32)
                long_v = d_ref[pl.ds(rows, 16), t * 128 : t * 128 + 128].astype(F32)
                back_g = d_ref[pl.ds(rows + 256, 16), t * 128 : t * 128 + 128].astype(F32)
                direct = long_v + skip * short_v
                gsg = c * direct
                gsv = skip * grad_long + back_g
                wv, wg = ahead(gsv), ahead(gsg)
                out_ref[piece, one, at] = (short_g * direct).astype(BF16)
                out_ref[piece, two, at] = (
                    tv[0] * gsv + tv[1] * jnp.where(lane > 126, nv[0], wv[0]) + tv[2] * jnp.where(lane > 125, nv[1], wv[1])
                ).astype(BF16)
                out_ref[piece, three, at] = (
                    tg[0] * gsg + tg[1] * jnp.where(lane > 126, ng[0], wg[0]) + tg[2] * jnp.where(lane > 125, ng[1], wg[1])
                ).astype(BF16)
                terms = (gsv * v, gsv * vb1, gsv * vb2, gsg * g, gsg * gb1, gsg * gb2, grad_long * short_v)
                acc = tuple(a + b for a, b in zip(acc, terms))
                v, v1, v2, g, g1, g2, nv, ng = pv, pv1, pv2, pg, pg1, pg2, wv, wg
            return (v, v1, v2), (g, g1, g2), nv, ng, acc

        last_v = r_ref[31, one, 128:256].astype(F32)
        last_g = r_ref[31, two, 128:256].astype(F32)
        zero = jnp.zeros((16, 128), F32)
        start = (
            (last_v, *rolled(last_v)),
            (last_g, *rolled(last_g)),
            ahead(next_ref[one, :]),
            ahead(next_ref[two, :]),
            (zero,) * 7,
        )
        acc = lax.fori_loop(0, 8, block, start)[4]
        total = zero
        for k in range(7):
            total = jnp.where(lane == k, jnp.sum(acc[k], axis=1, keepdims=True), total)
        sums_ref[one, :] = total


def call(kernel, outs, scratch, flops, moved, *args):
    vmem = pl.BlockSpec(memory_space=pltpu.VMEM)
    return pl.pallas_call(
        kernel,
        in_specs=[vmem] * len(args),
        out_specs=[vmem] * len(outs),
        compiler_params=pltpu.CompilerParams(vmem_limit_bytes=GRANT),
        out_shape=[jax.ShapeDtypeStruct(s, d) for s, d in outs],
        scratch_shapes=[pltpu.VMEM(s, d) for s, d in scratch],
        cost_estimate=pl.CostEstimate(flops=flops, bytes_accessed=moved, transcendentals=0),
    )(*args)


def spread(r, rim, cols, twiddle, cas):
    return call(spread_kernel, [((16, 256, 128), BF16)], [((512, 1024), BF16)], 1 << 30, 5 << 20, r, rim, cols, twiddle, cas)[0]


def mix(by_freq, spectrum, mixing):
    return call(
        mix_kernel,
        [((32, 64, 128), F32), ((16, 256, 128), BF16)],
        [((2048, 128), F32), ((2048, 128), F32)],
        1 << 30,
        5 << 20,
        by_freq,
        spectrum,
        mixing,
    )


def back(returned, r, rim, cols, twiddle, cas):
    return call(
        back_kernel,
        [((512, 1024), BF16), ((64, 128), F32)],
        [((512, 1024), BF16)],
        1 << 30,
        5 << 20,
        returned,
        r,
        rim,
        cols,
        twiddle,
        cas,
    )


def final(d, r, rim, following, cols):
    return call(
        final_kernel, [((32, 96, 256), BF16), ((32, 128), F32)], [], 1 << 24, 5 << 20, d, r, rim, following, cols
    )


def gather(*fields):
    return pl.pallas_call(
        gather_kernel,
        in_specs=[pl.BlockSpec(memory_space=pltpu.HBM)] * 3,
        out_specs=pl.BlockSpec(memory_space=pltpu.VMEM),
        out_shape=jax.ShapeDtypeStruct((32, 96, 256), BF16),
        scratch_shapes=[pltpu.SemaphoreType.DMA((3,))],
        compiler_params=pltpu.CompilerParams(vmem_limit_bytes=GRANT),
    )(*fields)


def exchange(array, axis):
    return lax.all_to_all(array, axis, 0, 0, tiled=True)


def per_device(values, gates, cotangent, taps_values, taps_gates, skip_gain, twiddle, mixing, spectrum):
    batch = lax.axis_size("batch")
    cas = jnp.asarray(cas_table())
    raw = gather(*(x.reshape(32, 32, 256) for x in (values, gates, cotangent)))
    r = exchange(raw, "seq")
    gains = jnp.concatenate([taps_values, taps_gates, skip_gain[None]], axis=0)
    cols = lax.dynamic_slice(gains, (0, lax.axis_index("seq") * 32), (7, 32))
    cols = jnp.pad(cols.T, ((0, 0), (0, 121)))
    rim = lax.ppermute(r[31, :64, 128:], "batch", [(i, i + 1) for i in range(batch - 1)])
    by_freq = exchange(spread(r, rim, cols, twiddle, cas), "batch")
    grad_spectrum, weighted = mix(by_freq, spectrum.transpose(0, 2, 1), mixing)
    d, head = back(exchange(weighted, "batch"), r, rim, cols, twiddle, cas)
    following = lax.ppermute(head, "batch", [(i + 1, i) for i in range(batch - 1)])
    done, sums = final(d, r, rim, following, cols)
    outs = exchange(done, "seq")
    step = 1
    while step < batch:
        sums = sums + lax.ppermute(sums, "batch", [(i, i ^ step) for i in range(batch)])
        step *= 2
    sums = sums[:, :7].T
    mixed, grad_values, grad_gates = (outs[:, k * 32 : k * 32 + 32].reshape(values.shape) for k in range(3))
    return mixed, grad_values, grad_gates, grad_spectrum.transpose(0, 2, 1), sums[0:3], sums[3:6], sums[6]


def solution(mesh):
    in_specs = (
        P(None, ("batch", "seq")),
        P(None, ("batch", "seq")),
        P(None, ("batch", "seq")),
        P(),
        P(),
        P(),
        P("batch", None),
        P(),
        P("seq", None, "batch"),
    )
    out_specs = (
        P(None, ("batch", "seq")),
        P(None, ("batch", "seq")),
        P(None, ("batch", "seq")),
        P("seq", None, "batch"),
        P(None, "seq"),
        P(None, "seq"),
        P("seq"),
    )
    return jax.shard_map(per_device, mesh=mesh, in_specs=in_specs, out_specs=out_specs, check_vma=False)
```

```python
import functools
import math

import jax
import jax.numpy as jnp
import numpy as np
from jax import lax
from jax.experimental import pallas as pl
from jax.experimental.pallas import tpu as pltpu
from jax.sharding import PartitionSpec as P

BLOCK = 1024
F32, BF16 = jnp.float32, jnp.bfloat16
GRANT = 20 << 20
PARTS = 4


def cas_table():
    indices = np.arange(BLOCK, dtype=np.int32)
    products = indices[:, None] * indices[None, :] % BLOCK
    angles = products.astype(np.float32) * np.float32(2.0 * math.pi / BLOCK)
    table = (np.cos(angles) + np.sin(angles)) / np.float32(math.sqrt(BLOCK))
    return table.astype(jnp.bfloat16)


def lanes(shape=(32, 128)):
    return lax.broadcasted_iota(jnp.int32, shape, 1)


def back_in_time(now, before, steps, lane):
    return jnp.where(lane < steps, before, now)


def rolled(tile):
    return pltpu.roll(tile, 1, 1), pltpu.roll(tile, 2, 1)


def column(cols, at):
    return jnp.broadcast_to(cols[:, at : at + 1], (cols.shape[0], 128))


def gather_kernel(a_ref, b_ref, c_ref, out_ref, held, in_sems, out_sems):
    size = 32 // PARTS
    arrive, leave = [], []
    for p in range(PARTS):
        own = slice(p * size, p * size + size)
        arrive.append(
            [
                pltpu.make_async_copy(ref.at[own], held.at[own, k * 32 : k * 32 + 32, :], in_sems.at[p, k])
                for k, ref in enumerate((a_ref, b_ref, c_ref))
            ]
        )
        leave.append(pltpu.make_async_copy(held.at[own], out_ref.at[own], out_sems.at[p]))
    for part in arrive:
        for copy in part:
            copy.start()
    for part, copy in zip(arrive, leave):
        for one in part:
            one.wait()
        copy.start()
    for copy in leave:
        copy.wait()


def keep_kernel(table_ref, out_ref, sem):
    copy = pltpu.make_async_copy(table_ref, out_ref, sem)
    copy.start()
    copy.wait()


def spread_kernel(r_ref, rim_ref, cols_ref, tw_ref, cas_ref, out_ref, lhs):
    lane = lanes((16, 128))
    for h in range(2):
        own = slice(h * 16, h * 16 + 16)
        cols = cols_ref[own, :]
        tv = [column(cols, k) for k in range(3)]
        tg = [column(cols, 3 + k) for k in range(3)]

        def block(i, carry):
            v1, v2, g1, g2 = carry
            rows = pl.multiple_of(i * 32, 32) + h * 16
            for t in range(8):
                piece, at = i * 4 + t // 2, slice((t % 2) * 128, (t % 2) * 128 + 128)
                v = r_ref[piece, own, at].astype(F32)
                g = r_ref[piece, h * 16 + 32 : h * 16 + 48, at].astype(F32)
                c = r_ref[piece, h * 16 + 64 : h * 16 + 80, at].astype(F32)
                nv1, nv2 = rolled(v)
                ng1, ng2 = rolled(g)
                short_v = tv[0] * v + tv[1] * back_in_time(nv1, v1, 1, lane) + tv[2] * back_in_time(nv2, v2, 2, lane)
                short_g = tg[0] * g + tg[1] * back_in_time(ng1, g1, 1, lane) + tg[2] * back_in_time(ng2, g2, 2, lane)
                lhs[pl.ds(rows, 16), t * 128 : t * 128 + 128] = short_v.astype(BF16)
                lhs[pl.ds(rows + 256, 16), t * 128 : t * 128 + 128] = (c * short_g).astype(BF16)
                v1, v2, g1, g2 = nv1, nv2, ng1, ng2
            return v1, v2, g1, g2

        start = rolled(rim_ref[own, :].astype(F32)) + rolled(rim_ref[h * 16 + 32 : h * 16 + 48, :].astype(F32))
        lax.fori_loop(0, 8, block, start)

    low = lanes((16, 128)) < 64

    def strip(n, _):
        at = pl.multiple_of(n * 256, 256)
        sums = jnp.dot(lhs[...], cas_ref[:, pl.ds(at, 256)], preferred_element_type=F32)
        for h in range(2):
            tw = tw_ref[:, pl.ds(pl.multiple_of(at + h * 128, 128), 128)]
            d = 4 * n + 2 * h
            for m in range(16):
                part = sums[m * 32 : m * 32 + 32, h * 128 : h * 128 + 128] * tw[m % 8 : m % 8 + 1, :]
                a, b = part[:16], part[16:]
                even = jnp.where(low, a, pltpu.roll(b, 64, 1))
                odd = jnp.where(low, pltpu.roll(a, 64, 1), b)
                out_ref[d, m * 16 : m * 16 + 16, :] = even.astype(BF16)
                out_ref[d + 1, m * 16 : m * 16 + 16, :] = odd.astype(BF16)
        return 0

    lax.fori_loop(0, 4, strip, 0)


def mix_kernel(f_ref, spec_ref, mix_ref, gs_ref, out_ref, wide_v, wide_g):
    wide = (wide_v, wide_g)
    for f in range(2):
        for b in range(16):
            wide[f][b * 128 : b * 128 + 128, :] = f_ref[b, f * 128 : f * 128 + 128, :].astype(F32)
    mixing = mix_ref[...]
    turned = mixing.T
    high = turned.astype(BF16)
    low = (turned - high.astype(F32)).astype(BF16)
    ahead = jnp.concatenate([high, low], axis=1)
    again = jnp.concatenate([jnp.concatenate([high, high], axis=1), jnp.concatenate([low, low], axis=1)], axis=0)

    for c in range(16):
        slabs = [wide[f][pl.ds(c, 128, stride=16), :].T.astype(BF16) for f in range(2)]
        both = jnp.dot(jnp.concatenate(slabs, axis=0), ahead, preferred_element_type=F32)
        both = both[:, :128] + both[:, 128:]
        sv, sg = both[:128], both[128:]
        filters = jnp.concatenate([spec_ref[c], spec_ref[16 + c]], axis=0).astype(F32)
        grad = sv * sg
        gs_ref[c] = grad[:64]
        gs_ref[16 + c] = grad[64:]
        product = jnp.concatenate([sv * filters, sg * filters], axis=0)
        top = product.astype(BF16)
        rest = (product - top.astype(F32)).astype(BF16)
        product = jnp.concatenate([top, rest], axis=1)
        sums = lax.dot_general(again, product, (((1,), (1,)), ((), ())), preferred_element_type=F32)
        sums = sums[:128] + sums[128:]
        for f in range(2):
            wide[f][pl.ds(c, 128, stride=16), :] = sums[:, f * 128 : f * 128 + 128]
    for f in range(2):
        wide[f][2048:2064, :] = jnp.zeros((16, 128), F32)
        for b in range(16):
            out_ref[b, f * 144 : f * 144 + 144, :] = wide[f][b * 128 : b * 128 + 144, :].astype(BF16)


def final_kernel(y_ref, r_ref, rim_ref, next_ref, cols_ref, tw_ref, cas_ref, out_ref, sums_ref, lhs, d_ref):
    low = lanes((16, 128)) < 64

    def unpack(y, _):
        at = pl.multiple_of(y * 128, 128)
        tw = tw_ref[:, pl.ds(at, 128)]
        for m in range(18):
            e = y_ref[2 * y, m * 16 : m * 16 + 16, :].astype(F32)
            o = y_ref[2 * y + 1, m * 16 : m * 16 + 16, :].astype(F32)
            row = tw[m % 9 : m % 9 + 1, :]
            a = jnp.where(low, e, pltpu.roll(o, 64, 1)) * row
            b = jnp.where(low, pltpu.roll(e, 64, 1), o) * row
            lhs[m * 32 : m * 32 + 16, pl.ds(at, 128)] = a.astype(BF16)
            lhs[m * 32 + 16 : m * 32 + 32, pl.ds(at, 128)] = b.astype(BF16)
        return 0

    lax.fori_loop(0, 8, unpack, 0)

    def strip(n, _):
        at = pl.multiple_of(n * 256, 256)
        sums = jnp.dot(lhs[...], cas_ref[:, pl.ds(at, 256)], preferred_element_type=F32)
        d_ref[:, pl.ds(at, 256)] = sums.astype(BF16)
        return 0

    lax.fori_loop(0, 4, strip, 0)

    lane = lanes((16, 128))

    def ahead(tile):
        return pltpu.roll(tile, 127, 1), pltpu.roll(tile, 126, 1)

    for h in range(2):
        one, two, three = (slice(h * 16 + k * 32, h * 16 + k * 32 + 16) for k in range(3))
        cols = cols_ref[one, :]
        tv = [column(cols, k) for k in range(3)]
        tg = [column(cols, 3 + k) for k in range(3)]
        skip = column(cols, 6)

        def block(step, carry):
            i = 7 - step
            (v, v1, v2), (g, g1, g2), nv, ng, acc = carry
            rows = pl.multiple_of(i * 32, 32) + h * 16
            for t in reversed(range(8)):
                piece, at = i * 4 + t // 2, slice((t % 2) * 128, (t % 2) * 128 + 128)
                if t > 0:
                    piece_b, at_b = i * 4 + (t - 1) // 2, slice(((t - 1) % 2) * 128, ((t - 1) % 2) * 128 + 128)
                    pv = r_ref[piece_b, one, at_b].astype(F32)
                    pg = r_ref[piece_b, two, at_b].astype(F32)
                else:
                    inside = i > 0
                    piece_b = jnp.maximum(i * 4 - 1, 0)
                    pv = jnp.where(inside, r_ref[piece_b, one, 128:256].astype(F32), rim_ref[one, :].astype(F32))
                    pg = jnp.where(inside, r_ref[piece_b, two, 128:256].astype(F32), rim_ref[two, :].astype(F32))
                pv1, pv2 = rolled(pv)
                pg1, pg2 = rolled(pg)
                vb1, vb2 = back_in_time(v1, pv1, 1, lane), back_in_time(v2, pv2, 2, lane)
                gb1, gb2 = back_in_time(g1, pg1, 1, lane), back_in_time(g2, pg2, 2, lane)
                short_v = (tv[0] * v + tv[1] * vb1 + tv[2] * vb2).astype(BF16).astype(F32)
                short_g = tg[0] * g + tg[1] * gb1 + tg[2] * gb2
                c = r_ref[piece, three, at].astype(F32)
                grad_long = (c * short_g).astype(BF16).astype(F32)
                long_v = d_ref[pl.ds(rows, 16), t * 128 : t * 128 + 128].astype(F32)
                back_g = d_ref[pl.ds(rows + 288, 16), t * 128 : t * 128 + 128].astype(F32)
                direct = long_v + skip * short_v
                gsg = c * direct
                gsv = skip * grad_long + back_g
                wv, wg = ahead(gsv), ahead(gsg)
                out_ref[piece, one, at] = (short_g * direct).astype(BF16)
                out_ref[piece, two, at] = (
                    tv[0] * gsv + tv[1] * jnp.where(lane > 126, nv[0], wv[0]) + tv[2] * jnp.where(lane > 125, nv[1], wv[1])
                ).astype(BF16)
                out_ref[piece, three, at] = (
                    tg[0] * gsg + tg[1] * jnp.where(lane > 126, ng[0], wg[0]) + tg[2] * jnp.where(lane > 125, ng[1], wg[1])
                ).astype(BF16)
                terms = (gsv * v, gsv * vb1, gsv * vb2, gsg * g, gsg * gb1, gsg * gb2, grad_long * short_v)
                acc = tuple(a + b for a, b in zip(acc, terms))
                v, v1, v2, g, g1, g2, nv, ng = pv, pv1, pv2, pg, pg1, pg2, wv, wg
            return (v, v1, v2), (g, g1, g2), nv, ng, acc

        last_v = r_ref[31, one, 128:256].astype(F32)
        last_g = r_ref[31, two, 128:256].astype(F32)
        next_v, next_g, next_c = (next_ref[rows, :].astype(F32) for rows in (one, two, three))
        short_v, short_g = tv[0] * next_v, tg[0] * next_g
        for k in (1, 2):
            short_v += tv[k] * back_in_time(pltpu.roll(next_v, k, 1), pltpu.roll(last_v, k, 1), k, lane)
            short_g += tg[k] * back_in_time(pltpu.roll(next_g, k, 1), pltpu.roll(last_g, k, 1), k, lane)
        short_v = short_v.astype(BF16).astype(F32)
        grad_long = (next_c * short_g).astype(BF16).astype(F32)
        long_v = d_ref[h * 16 + 256 : h * 16 + 272, 0:128].astype(F32)
        back_g = d_ref[h * 16 + 544 : h * 16 + 560, 0:128].astype(F32)
        zero = jnp.zeros((16, 128), F32)
        start = (
            (last_v, *rolled(last_v)),
            (last_g, *rolled(last_g)),
            ahead(skip * grad_long + back_g),
            ahead(next_c * (long_v + skip * short_v)),
            (zero,) * 7,
        )
        acc = lax.fori_loop(0, 8, block, start)[4]
        total = zero
        for k in range(7):
            total = jnp.where(lane == k, jnp.sum(acc[k], axis=1, keepdims=True), total)
        sums_ref[one, :] = total


def call(kernel, outs, scratch, flops, moved, *args):
    vmem = pl.BlockSpec(memory_space=pltpu.VMEM)
    return pl.pallas_call(
        kernel,
        in_specs=[vmem] * len(args),
        out_specs=[vmem] * len(outs),
        compiler_params=pltpu.CompilerParams(vmem_limit_bytes=GRANT),
        out_shape=[jax.ShapeDtypeStruct(s, d) for s, d in outs],
        scratch_shapes=[pltpu.VMEM(s, d) for s, d in scratch],
        cost_estimate=pl.CostEstimate(flops=flops, bytes_accessed=moved, transcendentals=0),
    )(*args)


def spread(r, rim, cols, twiddle, cas):
    return call(spread_kernel, [((16, 256, 128), BF16)], [((512, 1024), BF16)], 1 << 30, 5 << 20, r, rim, cols, twiddle, cas)[0]


def mix(by_freq, spectrum, mixing):
    return call(
        mix_kernel,
        [((32, 64, 128), F32), ((16, 288, 128), BF16)],
        [((2064, 128), F32), ((2064, 128), F32)],
        1 << 30,
        5 << 20,
        by_freq,
        spectrum,
        mixing,
    )


def final(returned, r, rim, following, cols, twiddle, cas):
    return call(
        final_kernel,
        [((32, 96, 256), BF16), ((32, 128), F32)],
        [((576, 1024), BF16), ((576, 1024), BF16)],
        1 << 30,
        8 << 20,
        returned,
        r,
        rim,
        following,
        cols,
        twiddle,
        cas,
    )


def gather(*fields):
    return pl.pallas_call(
        gather_kernel,
        in_specs=[pl.BlockSpec(memory_space=pl.ANY)] * 3,
        out_specs=pl.BlockSpec(memory_space=pl.ANY),
        out_shape=jax.ShapeDtypeStruct((32, 96, 256), BF16),
        scratch_shapes=[
            pltpu.VMEM((32, 96, 256), BF16),
            pltpu.SemaphoreType.DMA((PARTS, 3)),
            pltpu.SemaphoreType.DMA((PARTS,)),
        ],
    )(*fields)


def keep(table):
    return pl.pallas_call(
        keep_kernel,
        in_specs=[pl.BlockSpec(memory_space=pl.ANY)],
        out_specs=pl.BlockSpec(memory_space=pltpu.VMEM),
        out_shape=jax.ShapeDtypeStruct(table.shape, table.dtype),
        scratch_shapes=[pltpu.SemaphoreType.DMA(())],
        compiler_params=pltpu.CompilerParams(vmem_limit_bytes=GRANT),
        cost_estimate=pl.CostEstimate(flops=0, bytes_accessed=4 << 20, transcendentals=0),
    )(table)


def last_columns(values, gates):
    batch, seq = lax.axis_size("batch"), lax.axis_size("seq")
    axes = ("batch", "seq")
    rows = jnp.concatenate([values[:, -2:], gates[:, -2:]], axis=1).T
    half = seq // 2
    held = sum(
        lax.ppermute(rows, axes, [(b * seq + seq - 1, (b + 1) * seq + at) for b in range(batch - 1)]) for at in (0, half)
    )
    step = half // 2
    while step:
        held = held + lax.ppermute(held, "seq", [(at, at + step) for at in range(0, seq, 2 * step)])
        step //= 2
    own = lax.dynamic_slice(held, (0, lax.axis_index("seq") * 32), (4, 32))
    own = jnp.concatenate([own[:2].T, own[2:].T], axis=0)
    return jnp.pad(own, ((0, 0), (126, 0)))


def exchange(array, axis):
    return lax.all_to_all(array, axis, 0, 0, tiled=True)


def per_device(values, gates, cotangent, taps_values, taps_gates, skip_gain, twiddle, mixing, spectrum):
    batch = lax.axis_size("batch")
    raw = gather(*(x.reshape(32, 32, 256) for x in (values, gates, cotangent)))
    r = exchange(raw, "seq")
    cas = keep(jnp.asarray(cas_table()))
    rim = last_columns(values, gates)
    gains = jnp.concatenate([taps_values, taps_gates, skip_gain[None]], axis=0)
    cols = lax.dynamic_slice(gains, (0, lax.axis_index("seq") * 32), (7, 32))
    cols = jnp.pad(cols.T, ((0, 0), (0, 121)))
    by_freq = exchange(spread(r, rim, cols, twiddle, cas), "batch")
    behind = [(i + 1, i) for i in range(batch - 1)]
    first, row = lax.optimization_barrier((r[0, :, :128], twiddle[:1]))
    following = lax.ppermute(first, "batch", behind)
    rows = jnp.concatenate([twiddle, lax.ppermute(row, "batch", behind)], axis=0)
    grad_spectrum, weighted = mix(by_freq, spectrum.transpose(0, 2, 1), mixing)
    done, sums = final(exchange(weighted, "batch"), r, rim, following, cols, rows, cas)
    outs = exchange(done, "seq")
    step = 1
    while step < batch:
        sums = sums + lax.ppermute(sums, "batch", [(i, i ^ step) for i in range(batch)])
        step *= 2
    sums = sums[:, :7].T
    mixed, grad_values, grad_gates = (outs[:, k * 32 : k * 32 + 32].reshape(values.shape) for k in range(3))
    return mixed, grad_values, grad_gates, grad_spectrum.transpose(0, 2, 1), sums[0:3], sums[3:6], sums[6]


def solution(mesh):
    in_specs = (
        P(None, ("batch", "seq")),
        P(None, ("batch", "seq")),
        P(None, ("batch", "seq")),
        P(),
        P(),
        P(),
        P("batch", None),
        P(),
        P("seq", None, "batch"),
    )
    out_specs = (
        P(None, ("batch", "seq")),
        P(None, ("batch", "seq")),
        P(None, ("batch", "seq")),
        P("seq", None, "batch"),
        P(None, "seq"),
        P(None, "seq"),
        P("seq"),
    )
    return jax.shard_map(per_device, mesh=mesh, in_specs=in_specs, out_specs=out_specs, check_vma=False)
```

```python
import math

import jax
import jax.numpy as jnp
import numpy as np
from jax import lax
from jax.experimental import pallas as pl
from jax.experimental.pallas import tpu as pltpu
from jax.sharding import PartitionSpec as P


BLOCK = 1024
F32, BF16 = jnp.float32, jnp.bfloat16
GRANT = 20 << 20
PARTS = 4


def cas_table():
    indices = np.arange(BLOCK, dtype=np.int32)
    products = indices[:, None] * indices[None, :] % BLOCK
    angles = products.astype(np.float32) * np.float32(2.0 * math.pi / BLOCK)
    table = (np.cos(angles) + np.sin(angles)) / np.float32(math.sqrt(BLOCK))
    return table.astype(jnp.bfloat16)


def lanes(shape=(32, 128)):
    return lax.broadcasted_iota(jnp.int32, shape, 1)


def back_in_time(now, before, steps, lane):
    return jnp.where(lane < steps, before, now)


def rolled(tile):
    return pltpu.roll(tile, 1, 1), pltpu.roll(tile, 2, 1)


def column(cols, at):
    return jnp.broadcast_to(cols[:, at : at + 1], (cols.shape[0], 128))


def gather_kernel(a_ref, b_ref, c_ref, out_ref, held, in_sems, out_sems):
    size = 32 // PARTS
    arrive, leave = [], []
    for p in range(PARTS):
        own = slice(p * size, p * size + size)
        arrive.append(
            [
                pltpu.make_async_copy(ref.at[own], held.at[own, k * 32 : k * 32 + 32, :], in_sems.at[p, k])
                for k, ref in enumerate((a_ref, b_ref, c_ref))
            ]
        )
        leave.append(pltpu.make_async_copy(held.at[own], out_ref.at[own], out_sems.at[p]))
    for part in arrive:
        for copy in part:
            copy.start()
    for part, copy in zip(arrive, leave):
        for one in part:
            one.wait()
        copy.start()
    for copy in leave:
        copy.wait()


def keep_kernel(table_ref, out_ref, sem):
    copy = pltpu.make_async_copy(table_ref, out_ref, sem)
    copy.start()
    copy.wait()


def shorten(tile, one, two, taps):
    return taps[0] * tile + taps[1] * one + taps[2] * two


def local_kernel(r_ref, cols_ref, lhs_ref):
    lane = lanes((16, 128))
    zero = jnp.zeros((16, 128), F32)
    for h in range(2):
        one, two, three = (slice(h * 16 + k * 32, h * 16 + k * 32 + 16) for k in range(3))
        cols = cols_ref[one, :]
        tv = [column(cols, k) for k in range(3)]
        tg = [column(cols, 3 + k) for k in range(3)]

        def block(i, carry):
            v1, v2, g1, g2 = carry
            rows = pl.multiple_of(i * 32, 32) + h * 16
            for t in range(8):
                piece, at = i * 4 + t // 2, slice((t % 2) * 128, (t % 2) * 128 + 128)
                v = r_ref[piece, one, at].astype(F32)
                g = r_ref[piece, two, at].astype(F32)
                c = r_ref[piece, three, at].astype(F32)
                nv1, nv2 = rolled(v)
                ng1, ng2 = rolled(g)
                short_v = shorten(v, back_in_time(nv1, v1, 1, lane), back_in_time(nv2, v2, 2, lane), tv)
                short_g = shorten(g, back_in_time(ng1, g1, 1, lane), back_in_time(ng2, g2, 2, lane), tg)
                lhs_ref[pl.ds(rows, 16), t * 128 : t * 128 + 128] = short_v.astype(BF16)
                lhs_ref[pl.ds(rows + 256, 16), t * 128 : t * 128 + 128] = (c * short_g).astype(BF16)
                v1, v2, g1, g2 = nv1, nv2, ng1, ng2
            return v1, v2, g1, g2

        lax.fori_loop(0, 8, block, (zero,) * 4)


def spread_kernel(part_ref, r_ref, rim_ref, cols_ref, tw_ref, cas_ref, out_ref, lhs):
    lane = lanes((16, 128))
    lhs[...] = part_ref[...]
    for h in range(2):
        one, two, three = (slice(h * 16 + k * 32, h * 16 + k * 32 + 16) for k in range(3))
        cols = cols_ref[one, :]
        short = []
        for k, own in enumerate((one, two)):
            tile = r_ref[0, own, 0:128].astype(F32)
            before = rolled(rim_ref[own, :].astype(F32))
            shifted = [back_in_time(a, b, n + 1, lane) for n, (a, b) in enumerate(zip(rolled(tile), before))]
            short.append(shorten(tile, *shifted, [column(cols, 3 * k + n) for n in range(3)]))
        lhs[one, 0:128] = short[0].astype(BF16)
        lhs[256 + h * 16 : 272 + h * 16, 0:128] = (r_ref[0, three, 0:128].astype(F32) * short[1]).astype(BF16)

    low = lanes((16, 128)) < 64

    def strip(n, _):
        at = pl.multiple_of(n * 256, 256)
        sums = jnp.dot(lhs[...], cas_ref[:, pl.ds(at, 256)], preferred_element_type=F32)
        for h in range(2):
            tw = tw_ref[:, pl.ds(pl.multiple_of(at + h * 128, 128), 128)]
            d = 4 * n + 2 * h
            for m in range(16):
                part = sums[m * 32 : m * 32 + 32, h * 128 : h * 128 + 128] * tw[m % 8 : m % 8 + 1, :]
                a, b = part[:16], part[16:]
                even = jnp.where(low, a, pltpu.roll(b, 64, 1))
                odd = jnp.where(low, pltpu.roll(a, 64, 1), b)
                out_ref[d, m * 16 : m * 16 + 16, :] = even.astype(BF16)
                out_ref[d + 1, m * 16 : m * 16 + 16, :] = odd.astype(BF16)
        return 0

    lax.fori_loop(0, 4, strip, 0)


def mix_kernel(f_ref, spec_ref, mix_ref, gs_ref, out_ref, wide_v, wide_g):
    wide = (wide_v, wide_g)
    for f in range(2):
        for b in range(16):
            wide[f][b * 128 : b * 128 + 128, :] = f_ref[b, f * 128 : f * 128 + 128, :].astype(F32)
    mixing = mix_ref[...]
    turned = mixing.T
    high = turned.astype(BF16)
    low = (turned - high.astype(F32)).astype(BF16)
    ahead = jnp.concatenate([high, low], axis=1)
    again = jnp.concatenate([jnp.concatenate([high, high], axis=1), jnp.concatenate([low, low], axis=1)], axis=0)

    for c in range(16):
        slabs = [wide[f][pl.ds(c, 128, stride=16), :].T.astype(BF16) for f in range(2)]
        both = jnp.dot(jnp.concatenate(slabs, axis=0), ahead, preferred_element_type=F32)
        both = both[:, :128] + both[:, 128:]
        sv, sg = both[:128], both[128:]
        filters = jnp.concatenate([spec_ref[c], spec_ref[16 + c]], axis=0).astype(F32)
        grad = sv * sg
        gs_ref[c] = grad[:64]
        gs_ref[16 + c] = grad[64:]
        product = jnp.concatenate([sv * filters, sg * filters], axis=0)
        top = product.astype(BF16)
        rest = (product - top.astype(F32)).astype(BF16)
        product = jnp.concatenate([top, rest], axis=1)
        sums = lax.dot_general(again, product, (((1,), (1,)), ((), ())), preferred_element_type=F32)
        sums = sums[:128] + sums[128:]
        for f in range(2):
            wide[f][pl.ds(c, 128, stride=16), :] = sums[:, f * 128 : f * 128 + 128]
    for f in range(2):
        for b in range(16):
            out_ref[b, f * 128 : f * 128 + 128, :] = wide[f][b * 128 : b * 128 + 128, :].astype(BF16)


def back_kernel(y_ref, r_ref, rim_ref, cols_ref, tw_ref, cas_ref, out_ref, head_ref, lhs):
    low = lanes((16, 128)) < 64

    def unpack(y, _):
        at = pl.multiple_of(y * 128, 128)
        tw = tw_ref[:, pl.ds(at, 128)]
        for m in range(16):
            e = y_ref[2 * y, m * 16 : m * 16 + 16, :].astype(F32)
            o = y_ref[2 * y + 1, m * 16 : m * 16 + 16, :].astype(F32)
            row = tw[m % 8 : m % 8 + 1, :]
            a = jnp.where(low, e, pltpu.roll(o, 64, 1)) * row
            b = jnp.where(low, pltpu.roll(e, 64, 1), o) * row
            lhs[m * 32 : m * 32 + 16, pl.ds(at, 128)] = a.astype(BF16)
            lhs[m * 32 + 16 : m * 32 + 32, pl.ds(at, 128)] = b.astype(BF16)
        return 0

    lax.fori_loop(0, 8, unpack, 0)

    def strip(n, _):
        at = pl.multiple_of(n * 256, 256)
        sums = jnp.dot(lhs[...], cas_ref[:, pl.ds(at, 256)], preferred_element_type=F32)
        out_ref[:, pl.ds(at, 256)] = sums.astype(BF16)
        return 0

    lax.fori_loop(0, 4, strip, 0)

    lane = lanes()
    cols = cols_ref[...]
    v, g, c = (r_ref[0, k * 32 : k * 32 + 32, 0:128].astype(F32) for k in range(3))
    before_v, before_g = rim_ref[0:32, :].astype(F32), rim_ref[32:64, :].astype(F32)
    short_v, short_g = v * column(cols, 0), g * column(cols, 3)
    for k in (1, 2):
        short_v += column(cols, k) * back_in_time(pltpu.roll(v, k, 1), pltpu.roll(before_v, k, 1), k, lane)
        short_g += column(cols, 3 + k) * back_in_time(pltpu.roll(g, k, 1), pltpu.roll(before_g, k, 1), k, lane)
    short_v = short_v.astype(BF16).astype(F32)
    grad_long = (c * short_g).astype(BF16).astype(F32)
    skip = column(cols, 6)
    head_ref[0:32, :] = skip * grad_long + out_ref[256:288, 0:128].astype(F32)
    head_ref[32:64, :] = c * (out_ref[0:32, 0:128].astype(F32) + skip * short_v)


def finish(r_ref, d_ref, rim_ref, cols_ref, stage, sums_ref, first, count, following, on_block):
    lane = lanes((16, 128))

    def ahead(tile):
        return pltpu.roll(tile, 127, 1), pltpu.roll(tile, 126, 1)

    for h in range(2):
        one, two, three = (slice(h * 16 + k * 32, h * 16 + k * 32 + 16) for k in range(3))
        cols = cols_ref[one, :]
        tv = [column(cols, k) for k in range(3)]
        tg = [column(cols, 3 + k) for k in range(3)]
        skip = column(cols, 6)

        def gradients(v, vb, g, gb, c, long_v, back_g):
            short_v = shorten(v, *vb, tv).astype(BF16).astype(F32)
            short_g = shorten(g, *gb, tg)
            grad_long = (c * short_g).astype(BF16).astype(F32)
            direct = long_v + skip * short_v
            return short_v, short_g, grad_long, direct, skip * grad_long + back_g, c * direct

        def block(step, carry):
            i = first + count - 1 - step
            (v, v1, v2), (g, g1, g2), nv, ng, acc = carry
            rows = pl.multiple_of(i * 32, 32) + h * 16
            for t in reversed(range(8)):
                piece, at = i * 4 + t // 2, slice((t % 2) * 128, (t % 2) * 128 + 128)
                if t > 0:
                    piece_b, at_b = i * 4 + (t - 1) // 2, slice(((t - 1) % 2) * 128, ((t - 1) % 2) * 128 + 128)
                    pv = r_ref[piece_b, one, at_b].astype(F32)
                    pg = r_ref[piece_b, two, at_b].astype(F32)
                else:
                    inside = i > 0
                    piece_b = jnp.maximum(i * 4 - 1, 0)
                    pv = jnp.where(inside, r_ref[piece_b, one, 128:256].astype(F32), rim_ref[one, :].astype(F32))
                    pg = jnp.where(inside, r_ref[piece_b, two, 128:256].astype(F32), rim_ref[two, :].astype(F32))
                pv1, pv2 = rolled(pv)
                pg1, pg2 = rolled(pg)
                vb = back_in_time(v1, pv1, 1, lane), back_in_time(v2, pv2, 2, lane)
                gb = back_in_time(g1, pg1, 1, lane), back_in_time(g2, pg2, 2, lane)
                c = r_ref[piece, three, at].astype(F32)
                long_v = d_ref[pl.ds(rows, 16), t * 128 : t * 128 + 128].astype(F32)
                back_g = d_ref[pl.ds(rows + 256, 16), t * 128 : t * 128 + 128].astype(F32)
                short_v, short_g, grad_long, direct, gsv, gsg = gradients(v, vb, g, gb, c, long_v, back_g)
                wv, wg = ahead(gsv), ahead(gsg)
                put = piece - first * 4
                stage[put, one, at] = (short_g * direct).astype(BF16)
                stage[put, two, at] = shorten(
                    gsv, jnp.where(lane > 126, nv[0], wv[0]), jnp.where(lane > 125, nv[1], wv[1]), tv
                ).astype(BF16)
                stage[put, three, at] = shorten(
                    gsg, jnp.where(lane > 126, ng[0], wg[0]), jnp.where(lane > 125, ng[1], wg[1]), tg
                ).astype(BF16)
                terms = (gsv * v, gsv * vb[0], gsv * vb[1], gsg * g, gsg * gb[0], gsg * gb[1], grad_long * short_v)
                acc = tuple(a + b for a, b in zip(acc, terms))
                v, v1, v2, g, g1, g2, nv, ng = pv, pv1, pv2, pg, pg1, pg2, wv, wg
            if h == 1:
                on_block(i - first)
            return (v, v1, v2), (g, g1, g2), nv, ng, acc

        end = first * 4 + count * 4 - 1
        last_v = r_ref[end, one, 128:256].astype(F32)
        last_g = r_ref[end, two, 128:256].astype(F32)
        last_v = last_v, *rolled(last_v)
        last_g = last_g, *rolled(last_g)
        if following is None:
            rows = (first + count) * 32 + h * 16
            next_v, next_g, c = (r_ref[end + 1, own, 0:128].astype(F32) for own in (one, two, three))
            vb = [back_in_time(a, b, n + 1, lane) for n, (a, b) in enumerate(zip(rolled(next_v), last_v[1:]))]
            gb = [back_in_time(a, b, n + 1, lane) for n, (a, b) in enumerate(zip(rolled(next_g), last_g[1:]))]
            long_v = d_ref[rows : rows + 16, 0:128].astype(F32)
            back_g = d_ref[rows + 256 : rows + 272, 0:128].astype(F32)
            gsv, gsg = gradients(next_v, vb, next_g, gb, c, long_v, back_g)[4:]
        else:
            gsv, gsg = following[one, :], following[two, :]
        zero = jnp.zeros((16, 128), F32)
        start = last_v, last_g, ahead(gsv), ahead(gsg), (zero,) * 7
        acc = lax.fori_loop(0, count, block, start)[4]
        total = zero
        for k in range(7):
            total = jnp.where(lane == k, jnp.sum(acc[k], axis=1, keepdims=True), total)
        sums_ref[one, :] = total


def most_kernel(d_ref, r_ref, rim_ref, cols_ref, out_ref, sums_ref, stage, sems):
    def leave(i):
        own = pl.ds(i * 4, 4)
        return pltpu.make_async_copy(stage.at[own], out_ref.at[own], sems.at[i])

    def on_block(i):
        leave(i).start()

    finish(r_ref, d_ref, rim_ref, cols_ref, stage, sums_ref, 0, 7, None, on_block)
    for i in range(7):
        leave(i).wait()


def last_kernel(most_ref, d_ref, r_ref, rim_ref, next_ref, cols_ref, some_ref, out_ref, sums_ref, stage, sem):
    finish(r_ref, d_ref, rim_ref, cols_ref, stage, sums_ref, 7, 1, next_ref, lambda i: None)
    copy = pltpu.make_async_copy(stage, out_ref.at[28:32], sem)
    copy.start()
    sums_ref[...] = sums_ref[...] + some_ref[...]
    copy.wait()


VMEM = pl.BlockSpec(memory_space=pltpu.VMEM)
ANY = pl.BlockSpec(memory_space=pl.ANY)


def call(kernel, outs, scratch, flops, moved, *args, **more):
    return pl.pallas_call(
        kernel,
        **{"in_specs": [VMEM] * len(args), "out_specs": [VMEM] * len(outs), **more},
        compiler_params=pltpu.CompilerParams(vmem_limit_bytes=GRANT),
        out_shape=[jax.ShapeDtypeStruct(s, d) for s, d in outs],
        scratch_shapes=[s if d is None else pltpu.VMEM(s, d) for s, d in scratch],
        cost_estimate=pl.CostEstimate(flops=flops, bytes_accessed=moved, transcendentals=0),
    )(*args)


def local(r, cols):
    return call(local_kernel, [((512, 1024), BF16)], [], 1 << 24, 4 << 20, r, cols)[0]


def spread(part, r, rim, cols, twiddle, cas):
    return call(
        spread_kernel,
        [((16, 256, 128), BF16)],
        [((512, 1024), BF16)],
        1 << 30,
        5 << 20,
        part,
        r,
        rim,
        cols,
        twiddle,
        cas,
    )[0]


def mix(by_freq, spectrum, mixing):
    return call(
        mix_kernel,
        [((32, 64, 128), F32), ((16, 256, 128), BF16)],
        [((2048, 128), F32), ((2048, 128), F32)],
        1 << 30,
        5 << 20,
        by_freq,
        spectrum,
        mixing,
    )


def back(returned, r, rim, cols, twiddle, cas):
    return call(
        back_kernel,
        [((512, 1024), BF16), ((64, 128), F32)],
        [((512, 1024), BF16)],
        1 << 30,
        5 << 20,
        returned,
        r,
        rim,
        cols,
        twiddle,
        cas,
    )


def most(d, r, rim, cols):
    return call(
        most_kernel,
        [((32, 96, 256), BF16), ((32, 128), F32)],
        [((28, 96, 256), BF16), (pltpu.SemaphoreType.DMA((7,)), None)],
        1 << 25,
        8 << 20,
        d,
        r,
        rim,
        cols,
        out_specs=[ANY, VMEM],
    )


def last(done, d, r, rim, following, cols, sums):
    return call(
        last_kernel,
        [((32, 96, 256), BF16), ((32, 128), F32)],
        [((4, 96, 256), BF16), (pltpu.SemaphoreType.DMA(()), None)],
        1 << 22,
        1 << 20,
        done,
        d,
        r,
        rim,
        following,
        cols,
        sums,
        in_specs=[ANY] + [VMEM] * 6,
        out_specs=[ANY, VMEM],
        input_output_aliases={0: 0},
    )


def gather(*fields):
    return pl.pallas_call(
        gather_kernel,
        in_specs=[pl.BlockSpec(memory_space=pl.ANY)] * 3,
        out_specs=pl.BlockSpec(memory_space=pl.ANY),
        out_shape=jax.ShapeDtypeStruct((32, 96, 256), BF16),
        scratch_shapes=[
            pltpu.VMEM((32, 96, 256), BF16),
            pltpu.SemaphoreType.DMA((PARTS, 3)),
            pltpu.SemaphoreType.DMA((PARTS,)),
        ],
    )(*fields)


def keep(table):
    return pl.pallas_call(
        keep_kernel,
        in_specs=[pl.BlockSpec(memory_space=pl.ANY)],
        out_specs=pl.BlockSpec(memory_space=pltpu.VMEM),
        out_shape=jax.ShapeDtypeStruct(table.shape, table.dtype),
        scratch_shapes=[pltpu.SemaphoreType.DMA(())],
        compiler_params=pltpu.CompilerParams(vmem_limit_bytes=GRANT),
        cost_estimate=pl.CostEstimate(flops=0, bytes_accessed=4 << 20, transcendentals=0),
    )(table)


def exchange(array, axis):
    return lax.all_to_all(array, axis, 0, 0, tiled=True)


def per_device(values, gates, cotangent, taps_values, taps_gates, skip_gain, twiddle, mixing, spectrum):
    batch = lax.axis_size("batch")
    raw = gather(*(x.reshape(32, 32, 256) for x in (values, gates, cotangent)))
    r = exchange(raw, "seq")
    cas = keep(jnp.asarray(cas_table()))
    gains = jnp.concatenate([taps_values, taps_gates, skip_gain[None]], axis=0)
    cols = lax.dynamic_slice(gains, (0, lax.axis_index("seq") * 32), (7, 32))
    cols = jnp.pad(cols.T, ((0, 0), (0, 121)))
    rim = lax.ppermute(r[31, :64, 128:], "batch", [(i, i + 1) for i in range(batch - 1)])
    by_freq = exchange(spread(local(r, cols), r, rim, cols, twiddle, cas), "batch")
    grad_spectrum, weighted = mix(by_freq, spectrum.transpose(0, 2, 1), mixing)
    d, head = back(exchange(weighted, "batch"), r, rim, cols, twiddle, cas)
    following = lax.ppermute(head, "batch", [(i + 1, i) for i in range(batch - 1)])
    done, sums = most(d, r, rim, cols)
    done, sums = last(done, d, r, rim, following, cols, sums)
    outs = exchange(done, "seq")
    step = 1
    while step < batch:
        sums = sums + lax.ppermute(sums, "batch", [(i, i ^ step) for i in range(batch)])
        step *= 2
    sums = sums[:, :7].T
    mixed, grad_values, grad_gates = (outs[:, k * 32 : k * 32 + 32].reshape(values.shape) for k in range(3))
    return mixed, grad_values, grad_gates, grad_spectrum.transpose(0, 2, 1), sums[0:3], sums[3:6], sums[6]


def solution(mesh):
    in_specs = (
        P(None, ("batch", "seq")),
        P(None, ("batch", "seq")),
        P(None, ("batch", "seq")),
        P(),
        P(),
        P(),
        P("batch", None),
        P(),
        P("seq", None, "batch"),
    )
    out_specs = (
        P(None, ("batch", "seq")),
        P(None, ("batch", "seq")),
        P(None, ("batch", "seq")),
        P("seq", None, "batch"),
        P(None, "seq"),
        P(None, "seq"),
        P("seq"),
    )
    return jax.shard_map(per_device, mesh=mesh, in_specs=in_specs, out_specs=out_specs, check_vma=False)
```

```python
import math

import jax
import jax.numpy as jnp
import numpy as np
from jax import lax
from jax.experimental import pallas as pl
from jax.experimental.pallas import tpu as pltpu
from jax.sharding import PartitionSpec as P


BLOCK = 1024
F32, BF16 = jnp.float32, jnp.bfloat16
GRANT = 20 << 20
PARTS = 4


def cas_table():
    indices = np.arange(BLOCK, dtype=np.int32)
    products = indices[:, None] * indices[None, :] % BLOCK
    angles = products.astype(np.float32) * np.float32(2.0 * math.pi / BLOCK)
    table = (np.cos(angles) + np.sin(angles)) / np.float32(math.sqrt(BLOCK))
    return table.astype(jnp.bfloat16)


def lanes(shape=(32, 128)):
    return lax.broadcasted_iota(jnp.int32, shape, 1)


def back_in_time(now, before, steps, lane):
    return jnp.where(lane < steps, before, now)


def rolled(tile):
    return pltpu.roll(tile, 1, 1), pltpu.roll(tile, 2, 1)


def column(cols, at):
    return jnp.broadcast_to(cols[:, at : at + 1], (cols.shape[0], 128))


def gather_kernel(a_ref, b_ref, c_ref, out_ref, held, in_sems, out_sems):
    size = 32 // PARTS
    arrive, leave = [], []
    for p in range(PARTS):
        own = slice(p * size, p * size + size)
        arrive.append(
            [
                pltpu.make_async_copy(ref.at[own], held.at[own, k * 32 : k * 32 + 32, :], in_sems.at[p, k])
                for k, ref in enumerate((a_ref, b_ref, c_ref))
            ]
        )
        leave.append(pltpu.make_async_copy(held.at[own], out_ref.at[own], out_sems.at[p]))
    for part in arrive:
        for copy in part:
            copy.start()
    for part, copy in zip(arrive, leave):
        for one in part:
            one.wait()
        copy.start()
    for copy in leave:
        copy.wait()


def keep_kernel(table_ref, out_ref, sem):
    copy = pltpu.make_async_copy(table_ref, out_ref, sem)
    copy.start()
    copy.wait()


def shorten(tile, one, two, taps):
    return taps[0] * tile + taps[1] * one + taps[2] * two


def local_kernel(r_ref, cols_ref, lhs_ref):
    lane = lanes((16, 128))
    zero = jnp.zeros((16, 128), F32)
    for h in range(2):
        one, two, three = (slice(h * 16 + k * 32, h * 16 + k * 32 + 16) for k in range(3))
        cols = cols_ref[one, :]
        tv = [column(cols, k) for k in range(3)]
        tg = [column(cols, 3 + k) for k in range(3)]

        def block(i, carry):
            v1, v2, g1, g2 = carry
            rows = pl.multiple_of(i * 32, 32) + h * 16
            for t in range(8):
                piece, at = i * 4 + t // 2, slice((t % 2) * 128, (t % 2) * 128 + 128)
                v = r_ref[piece, one, at].astype(F32)
                g = r_ref[piece, two, at].astype(F32)
                c = r_ref[piece, three, at].astype(F32)
                nv1, nv2 = rolled(v)
                ng1, ng2 = rolled(g)
                short_v = shorten(v, back_in_time(nv1, v1, 1, lane), back_in_time(nv2, v2, 2, lane), tv)
                short_g = shorten(g, back_in_time(ng1, g1, 1, lane), back_in_time(ng2, g2, 2, lane), tg)
                lhs_ref[pl.ds(rows, 16), t * 128 : t * 128 + 128] = short_v.astype(BF16)
                lhs_ref[pl.ds(rows + 256, 16), t * 128 : t * 128 + 128] = (c * short_g).astype(BF16)
                v1, v2, g1, g2 = nv1, nv2, ng1, ng2
            return v1, v2, g1, g2

        lax.fori_loop(0, 8, block, (zero,) * 4)


def spread_kernel(part_ref, r_ref, rim_ref, cols_ref, tw_ref, cas_ref, out_ref, lhs):
    lane = lanes((16, 128))
    lhs[...] = part_ref[...]
    for h in range(2):
        one, two, three = (slice(h * 16 + k * 32, h * 16 + k * 32 + 16) for k in range(3))
        cols = cols_ref[one, :]
        short = []
        for k, own in enumerate((one, two)):
            tile = r_ref[0, own, 0:128].astype(F32)
            before = rolled(rim_ref[own, :].astype(F32))
            shifted = [back_in_time(a, b, n + 1, lane) for n, (a, b) in enumerate(zip(rolled(tile), before))]
            short.append(shorten(tile, *shifted, [column(cols, 3 * k + n) for n in range(3)]))
        lhs[one, 0:128] = short[0].astype(BF16)
        lhs[256 + h * 16 : 272 + h * 16, 0:128] = (r_ref[0, three, 0:128].astype(F32) * short[1]).astype(BF16)

    low = lanes((16, 128)) < 64

    def strip(n, _):
        at = pl.multiple_of(n * 256, 256)
        sums = jnp.dot(lhs[...], cas_ref[:, pl.ds(at, 256)], preferred_element_type=F32)
        for h in range(2):
            tw = tw_ref[:, pl.ds(pl.multiple_of(at + h * 128, 128), 128)]
            d = 4 * n + 2 * h
            for m in range(16):
                part = sums[m * 32 : m * 32 + 32, h * 128 : h * 128 + 128] * tw[m % 8 : m % 8 + 1, :]
                a, b = part[:16], part[16:]
                even = jnp.where(low, a, pltpu.roll(b, 64, 1))
                odd = jnp.where(low, pltpu.roll(a, 64, 1), b)
                out_ref[d, m * 16 : m * 16 + 16, :] = even.astype(BF16)
                out_ref[d + 1, m * 16 : m * 16 + 16, :] = odd.astype(BF16)
        return 0

    lax.fori_loop(0, 4, strip, 0)


def mix_kernel(f_ref, spec_ref, mix_ref, gs_ref, out_ref, wide_v, wide_g):
    wide = (wide_v, wide_g)
    for f in range(2):
        for b in range(16):
            wide[f][b * 128 : b * 128 + 128, :] = f_ref[b, f * 128 : f * 128 + 128, :].astype(F32)
    mixing = mix_ref[...]
    turned = mixing.T
    high = turned.astype(BF16)
    low = (turned - high.astype(F32)).astype(BF16)
    ahead = jnp.concatenate([high, low], axis=1)
    again = jnp.concatenate([jnp.concatenate([high, high], axis=1), jnp.concatenate([low, low], axis=1)], axis=0)

    for c in range(16):
        slabs = [wide[f][pl.ds(c, 128, stride=16), :].T.astype(BF16) for f in range(2)]
        both = jnp.dot(jnp.concatenate(slabs, axis=0), ahead, preferred_element_type=F32)
        both = both[:, :128] + both[:, 128:]
        sv, sg = both[:128], both[128:]
        filters = jnp.concatenate([spec_ref[c], spec_ref[16 + c]], axis=0).astype(F32)
        grad = sv * sg
        gs_ref[c] = grad[:64]
        gs_ref[16 + c] = grad[64:]
        product = jnp.concatenate([sv * filters, sg * filters], axis=0)
        top = product.astype(BF16)
        rest = (product - top.astype(F32)).astype(BF16)
        product = jnp.concatenate([top, rest], axis=1)
        sums = lax.dot_general(again, product, (((1,), (1,)), ((), ())), preferred_element_type=F32)
        sums = sums[:128] + sums[128:]
        for f in range(2):
            wide[f][pl.ds(c, 128, stride=16), :] = sums[:, f * 128 : f * 128 + 128]
    for f in range(2):
        for b in range(16):
            out_ref[b, f * 128 : f * 128 + 128, :] = wide[f][b * 128 : b * 128 + 128, :].astype(BF16)


def back_kernel(y_ref, r_ref, rim_ref, cols_ref, tw_ref, cas_ref, out_ref, head_ref, lhs):
    low = lanes((16, 128)) < 64

    def unpack(y, _):
        at = pl.multiple_of(y * 128, 128)
        tw = tw_ref[:, pl.ds(at, 128)]
        for m in range(16):
            e = y_ref[2 * y, m * 16 : m * 16 + 16, :].astype(F32)
            o = y_ref[2 * y + 1, m * 16 : m * 16 + 16, :].astype(F32)
            row = tw[m % 8 : m % 8 + 1, :]
            a = jnp.where(low, e, pltpu.roll(o, 64, 1)) * row
            b = jnp.where(low, pltpu.roll(e, 64, 1), o) * row
            lhs[m * 32 : m * 32 + 16, pl.ds(at, 128)] = a.astype(BF16)
            lhs[m * 32 + 16 : m * 32 + 32, pl.ds(at, 128)] = b.astype(BF16)
        return 0

    lax.fori_loop(0, 8, unpack, 0)

    def strip(n, _):
        at = pl.multiple_of(n * 256, 256)
        sums = jnp.dot(lhs[...], cas_ref[:, pl.ds(at, 256)], preferred_element_type=F32)
        out_ref[:, pl.ds(at, 256)] = sums.astype(BF16)
        return 0

    lax.fori_loop(0, 4, strip, 0)

    lane = lanes()
    cols = cols_ref[...]
    v, g, c = (r_ref[0, k * 32 : k * 32 + 32, 0:128].astype(F32) for k in range(3))
    before_v, before_g = rim_ref[0:32, :].astype(F32), rim_ref[32:64, :].astype(F32)
    short_v, short_g = v * column(cols, 0), g * column(cols, 3)
    for k in (1, 2):
        short_v += column(cols, k) * back_in_time(pltpu.roll(v, k, 1), pltpu.roll(before_v, k, 1), k, lane)
        short_g += column(cols, 3 + k) * back_in_time(pltpu.roll(g, k, 1), pltpu.roll(before_g, k, 1), k, lane)
    short_v = short_v.astype(BF16).astype(F32)
    grad_long = (c * short_g).astype(BF16).astype(F32)
    skip = column(cols, 6)
    head_ref[0:32, :] = skip * grad_long + out_ref[256:288, 0:128].astype(F32)
    head_ref[32:64, :] = c * (out_ref[0:32, 0:128].astype(F32) + skip * short_v)


def finish(r_ref, d_ref, rim_ref, cols_ref, stage, heads, sums_ref, first, count, following, on_block):
    lane = lanes((16, 128))

    def ahead(tile):
        return pltpu.roll(tile, 127, 1), pltpu.roll(tile, 126, 1)

    for h in range(2):
        one, two, three = (slice(h * 16 + k * 32, h * 16 + k * 32 + 16) for k in range(3))
        cols = cols_ref[one, :]
        tv = [column(cols, k) for k in range(3)]
        tg = [column(cols, 3 + k) for k in range(3)]
        skip = column(cols, 6)

        def gradients(v, vb, g, gb, c, long_v, back_g):
            short_v = shorten(v, *vb, tv).astype(BF16).astype(F32)
            short_g = shorten(g, *gb, tg)
            grad_long = (c * short_g).astype(BF16).astype(F32)
            direct = long_v + skip * short_v
            return short_v, short_g, grad_long, direct, skip * grad_long + back_g, c * direct

        def block(step, carry):
            i = first + count - 1 - step
            (v, v1, v2), (g, g1, g2), nv, acc = carry
            rows = pl.multiple_of(i * 32, 32) + h * 16
            for t in reversed(range(8)):
                piece, at = i * 4 + t // 2, slice((t % 2) * 128, (t % 2) * 128 + 128)
                if t > 0:
                    piece_b, at_b = i * 4 + (t - 1) // 2, slice(((t - 1) % 2) * 128, ((t - 1) % 2) * 128 + 128)
                    pv = r_ref[piece_b, one, at_b].astype(F32)
                    pg = r_ref[piece_b, two, at_b].astype(F32)
                else:
                    inside = i > 0
                    piece_b = jnp.maximum(i * 4 - 1, 0)
                    pv = jnp.where(inside, r_ref[piece_b, one, 128:256].astype(F32), rim_ref[one, :].astype(F32))
                    pg = jnp.where(inside, r_ref[piece_b, two, 128:256].astype(F32), rim_ref[two, :].astype(F32))
                pv1, pv2 = rolled(pv)
                pg1, pg2 = rolled(pg)
                vb = back_in_time(v1, pv1, 1, lane), back_in_time(v2, pv2, 2, lane)
                gb = back_in_time(g1, pg1, 1, lane), back_in_time(g2, pg2, 2, lane)
                c = r_ref[piece, three, at].astype(F32)
                long_v = d_ref[pl.ds(rows, 16), t * 128 : t * 128 + 128].astype(F32)
                back_g = d_ref[pl.ds(rows + 256, 16), t * 128 : t * 128 + 128].astype(F32)
                short_v, _, grad_long, direct, gsv, gsg = gradients(v, vb, g, gb, c, long_v, back_g)
                wv = ahead(gsv)
                put = piece - first * 4
                stage[put, one, at] = direct.astype(BF16)
                stage[put, two, at] = shorten(
                    gsv, jnp.where(lane > 126, nv[0], wv[0]), jnp.where(lane > 125, nv[1], wv[1]), tv
                ).astype(BF16)
                if t % 2 == 0:
                    heads[pl.ds(pl.multiple_of(put * 32, 32) + h * 16, 16), :] = gsg.astype(BF16)
                terms = (gsv * v, gsv * vb[0], gsv * vb[1], gsg * g, gsg * gb[0], gsg * gb[1], grad_long * short_v)
                acc = tuple(a + b for a, b in zip(acc, terms))
                v, v1, v2, g, g1, g2, nv = pv, pv1, pv2, pg, pg1, pg2, wv
            if h == 1:
                on_block(i - first)
            return (v, v1, v2), (g, g1, g2), nv, acc

        end = first * 4 + count * 4 - 1
        last_v = r_ref[end, one, 128:256].astype(F32)
        last_g = r_ref[end, two, 128:256].astype(F32)
        last_v = last_v, *rolled(last_v)
        last_g = last_g, *rolled(last_g)
        if following is None:
            rows = (first + count) * 32 + h * 16
            next_v, next_g, c = (r_ref[end + 1, own, 0:128].astype(F32) for own in (one, two, three))
            vb = [back_in_time(a, b, n + 1, lane) for n, (a, b) in enumerate(zip(rolled(next_v), last_v[1:]))]
            gb = [back_in_time(a, b, n + 1, lane) for n, (a, b) in enumerate(zip(rolled(next_g), last_g[1:]))]
            long_v = d_ref[rows : rows + 16, 0:128].astype(F32)
            back_g = d_ref[rows + 256 : rows + 272, 0:128].astype(F32)
            gsv = gradients(next_v, vb, next_g, gb, c, long_v, back_g)[4]
        else:
            gsv = following[one, :]
        zero = jnp.zeros((16, 128), F32)
        start = last_v, last_g, ahead(gsv), (zero,) * 7
        acc = lax.fori_loop(0, count, block, start)[3]
        total = zero
        for k in range(7):
            total = jnp.where(lane == k, jnp.sum(acc[k], axis=1, keepdims=True), total)
        sums_ref[one, :] = total


def most_kernel(d_ref, r_ref, rim_ref, cols_ref, out_ref, sums_ref, heads_ref, stage, sems):
    def leave(i):
        own = pl.ds(i * 4, 4)
        return pltpu.make_async_copy(stage.at[own], out_ref.at[own, 0:64, :], sems.at[i])

    def on_block(i):
        leave(i).start()

    finish(r_ref, d_ref, rim_ref, cols_ref, stage, heads_ref, sums_ref, 0, 7, None, on_block)
    for i in range(7):
        leave(i).wait()


def last_kernel(
    most_ref, d_ref, r_ref, rim_ref, next_ref, cols_ref, some_ref, heads_ref, out_ref, sums_ref, stage, edges, held, sems
):
    finish(r_ref, d_ref, rim_ref, cols_ref, stage, held, sums_ref, 7, 1, next_ref, lambda i: None)
    copies = [
        pltpu.make_async_copy(stage, out_ref.at[28:32, 0:64, :], sems.at[0]),
        pltpu.make_async_copy(edges, out_ref.at[:, 64:72, :], sems.at[1]),
    ]
    copies[0].start()
    sums_ref[...] = sums_ref[...] + some_ref[...]
    held[128:160, :] = next_ref[32:64, :].astype(BF16)
    line = lax.broadcasted_iota(jnp.int32, (8, 128), 0)
    lane = lanes((8, 128))
    after = ((line < 2) & (lane == line)).astype(F32).astype(BF16)
    before = ((line > 1) & (line < 4) & (lane == line + 124)).astype(F32).astype(BF16)
    dims = (((1,), (1,)), ((), ()))
    edges[:, :, 128:256] = jnp.zeros((32, 8, 128), BF16)
    for j in range(8):
        if j < 6:
            ahead = heads_ref[j * 128 + 32 : j * 128 + 160, :]
        elif j == 6:
            ahead = jnp.concatenate([heads_ref[800:896, :], held[0:32, :]], axis=0)
        else:
            ahead = held[32:160, :]
        pieces = [r_ref[p, 32:64, 128:256] if p >= 0 else rim_ref[32:64, :] for p in range(4 * j - 1, 4 * j + 3)]
        rows = lax.dot_general(after, ahead, dims, preferred_element_type=F32)
        rows += lax.dot_general(before, jnp.concatenate(pieces, axis=0), dims, preferred_element_type=F32)
        for p in range(4 * j, 4 * j + 4):
            edges[p, :, 0:128] = rows.astype(BF16)
    copies[1].start()
    for copy in copies:
        copy.wait()


def home_kernel(
    u_ref, g_ref, c_ref, cols_ref, sel_ref, mixed_ref, gv_ref, gg_ref, stage_m, stage_g, turned, sems
):
    direct = pltpu.make_async_copy(u_ref.at[:, 32:64, :], gv_ref, sems.at[0, 2])
    direct.start()
    lane = lanes((16, 128))
    for j in range(2):
        edge = u_ref[j * 16 : j * 16 + 16, 64:72, 0:128].astype(F32).reshape(128, 128).astype(BF16)
        turned[j] = lax.dot_general(sel_ref[...], edge, (((1,), (1,)), ((), ())), preferred_element_type=F32)

    def leave(j):
        own = pl.ds(pl.multiple_of(j * 512, 512), 512)
        return (
            pltpu.make_async_copy(stage_m.at[own], mixed_ref.at[own], sems.at[j, 0]),
            pltpu.make_async_copy(stage_g.at[own], gg_ref.at[own], sems.at[j, 1]),
        )

    def half(j, _):
        for k in range(16):
            for h in range(2):
                q = j * 16 + k
                rows = pl.ds(pl.multiple_of(q * 32, 32) + h * 16, 16)
                own = slice(h * 16, h * 16 + 16)
                after0, after1, before2, before1 = (
                    jnp.broadcast_to(turned[j, own, k * 8 + n : k * 8 + n + 1], (16, 128)) for n in range(4)
                )
                cols = cols_ref[rows, :]
                tg = [column(cols, n) for n in range(3)]
                g, c, u = (
                    [ref[:, at : at + 128].astype(F32) for at in (0, 128)]
                    for ref in (g_ref.at[rows], c_ref.at[rows], u_ref.at[q, own])
                )
                ones, twos = zip(*(rolled(x) for x in g))
                one = jnp.where(lane < 1, before1, ones[0]), back_in_time(ones[1], ones[0], 1, lane)
                two = jnp.where(lane < 1, before2, back_in_time(twos[0], before1, 2, lane)), back_in_time(twos[1], twos[0], 2, lane)
                s = [a * b for a, b in zip(c, u)]
                left = [(pltpu.roll(x, 127, 1), pltpu.roll(x, 126, 1)) for x in s]
                next1 = jnp.where(lane > 126, left[1][0], left[0][0]), jnp.where(lane > 126, after0, left[1][0])
                next2 = (
                    jnp.where(lane > 125, left[1][1], left[0][1]),
                    jnp.where(lane > 126, after1, jnp.where(lane > 125, after0, left[1][1])),
                )
                for n, at in enumerate((0, 128)):
                    stage_m[rows, at : at + 128] = (shorten(g[n], one[n], two[n], tg) * u[n]).astype(BF16)
                    stage_g[rows, at : at + 128] = shorten(s[n], next1[n], next2[n], tg).astype(BF16)
        for copy in leave(j):
            copy.start()
        return 0

    lax.fori_loop(0, 2, half, 0)
    direct.wait()
    for j in range(2):
        for copy in leave(j):
            copy.wait()


VMEM = pl.BlockSpec(memory_space=pltpu.VMEM)
ANY = pl.BlockSpec(memory_space=pl.ANY)


def call(kernel, outs, scratch, flops, moved, *args, **more):
    return pl.pallas_call(
        kernel,
        **{"in_specs": [VMEM] * len(args), "out_specs": [VMEM] * len(outs), **more},
        compiler_params=pltpu.CompilerParams(vmem_limit_bytes=GRANT),
        out_shape=[jax.ShapeDtypeStruct(s, d) for s, d in outs],
        scratch_shapes=[s if d is None else pltpu.VMEM(s, d) for s, d in scratch],
        cost_estimate=pl.CostEstimate(flops=flops, bytes_accessed=moved, transcendentals=0),
    )(*args)


def local(r, cols):
    return call(local_kernel, [((512, 1024), BF16)], [], 1 << 24, 4 << 20, r, cols)[0]


def spread(part, r, rim, cols, twiddle, cas):
    return call(
        spread_kernel,
        [((16, 256, 128), BF16)],
        [((512, 1024), BF16)],
        1 << 30,
        5 << 20,
        part,
        r,
        rim,
        cols,
        twiddle,
        cas,
    )[0]


def mix(by_freq, spectrum, mixing):
    return call(
        mix_kernel,
        [((32, 64, 128), F32), ((16, 256, 128), BF16)],
        [((2048, 128), F32), ((2048, 128), F32)],
        1 << 30,
        5 << 20,
        by_freq,
        spectrum,
        mixing,
    )


def back(returned, r, rim, cols, twiddle, cas):
    return call(
        back_kernel,
        [((512, 1024), BF16), ((64, 128), F32)],
        [((512, 1024), BF16)],
        1 << 30,
        5 << 20,
        returned,
        r,
        rim,
        cols,
        twiddle,
        cas,
    )


def most(d, r, rim, cols):
    return call(
        most_kernel,
        [((32, 72, 256), BF16), ((32, 128), F32), ((896, 128), BF16)],
        [((28, 64, 256), BF16), (pltpu.SemaphoreType.DMA((7,)), None)],
        1 << 25,
        8 << 20,
        d,
        r,
        rim,
        cols,
        out_specs=[ANY, VMEM, VMEM],
    )


def last(done, d, r, rim, following, cols, sums, heads):
    return call(
        last_kernel,
        [((32, 72, 256), BF16), ((32, 128), F32)],
        [
            ((4, 64, 256), BF16),
            ((32, 8, 256), BF16),
            ((160, 128), BF16),
            (pltpu.SemaphoreType.DMA((2,)), None),
        ],
        1 << 22,
        1 << 20,
        done,
        d,
        r,
        rim,
        following,
        cols,
        sums,
        heads,
        in_specs=[ANY] + [VMEM] * 7,
        out_specs=[ANY, VMEM],
        input_output_aliases={0: 0},
    )


def home(u, gates, cotangent, cols, sel):
    return call(
        home_kernel,
        [((1024, 256), BF16), ((32, 32, 256), BF16), ((1024, 256), BF16)],
        [
            ((1024, 256), BF16),
            ((1024, 256), BF16),
            ((2, 32, 128), F32),
            (pltpu.SemaphoreType.DMA((2, 3)), None),
        ],
        1 << 24,
        6 << 20,
        u,
        gates,
        cotangent,
        cols,
        sel,
        out_specs=[ANY] * 3,
    )


def gather(*fields):
    return pl.pallas_call(
        gather_kernel,
        in_specs=[pl.BlockSpec(memory_space=pl.ANY)] * 3,
        out_specs=pl.BlockSpec(memory_space=pl.ANY),
        out_shape=jax.ShapeDtypeStruct((32, 96, 256), BF16),
        scratch_shapes=[
            pltpu.VMEM((32, 96, 256), BF16),
            pltpu.SemaphoreType.DMA((PARTS, 3)),
            pltpu.SemaphoreType.DMA((PARTS,)),
        ],
    )(*fields)


def keep(table):
    return pl.pallas_call(
        keep_kernel,
        in_specs=[pl.BlockSpec(memory_space=pl.ANY)],
        out_specs=pl.BlockSpec(memory_space=pltpu.VMEM),
        out_shape=jax.ShapeDtypeStruct(table.shape, table.dtype),
        scratch_shapes=[pltpu.SemaphoreType.DMA(())],
        compiler_params=pltpu.CompilerParams(vmem_limit_bytes=GRANT),
        cost_estimate=pl.CostEstimate(flops=0, bytes_accessed=4 << 20, transcendentals=0),
    )(table)


def exchange(array, axis):
    return lax.all_to_all(array, axis, 0, 0, tiled=True)


def per_device(values, gates, cotangent, taps_values, taps_gates, skip_gain, twiddle, mixing, spectrum):
    batch = lax.axis_size("batch")
    raw = gather(*(x.reshape(32, 32, 256) for x in (values, gates, cotangent)))
    r = exchange(raw, "seq")
    cas = keep(jnp.asarray(cas_table()))
    gains = jnp.concatenate([taps_values, taps_gates, skip_gain[None]], axis=0)
    cols = lax.dynamic_slice(gains, (0, lax.axis_index("seq") * 32), (7, 32))
    cols = jnp.pad(cols.T, ((0, 0), (0, 121)))
    rim = lax.ppermute(r[31, :64, 128:], "batch", [(i, i + 1) for i in range(batch - 1)])
    by_freq = exchange(spread(local(r, cols), r, rim, cols, twiddle, cas), "batch")
    grad_spectrum, weighted = mix(by_freq, spectrum.transpose(0, 2, 1), mixing)
    d, head = back(exchange(weighted, "batch"), r, rim, cols, twiddle, cas)
    following = lax.ppermute(head, "batch", [(i + 1, i) for i in range(batch - 1)])
    done, sums, heads = most(d, r, rim, cols)
    done, sums = last(done, d, r, rim, following, cols, sums, heads)
    outs = exchange(done, "seq")
    gate_cols = jnp.pad(taps_gates.T, ((0, 0), (0, 125)))
    own = lax.rem(lax.axis_index("seq"), 4) * 32 + lax.broadcasted_iota(jnp.int32, (32, 128), 0)
    sel = (own == lanes()).astype(BF16)
    mixed, grad_values, grad_gates = home(outs, gates, cotangent, gate_cols, sel)
    step = 1
    while step < batch:
        sums = sums + lax.ppermute(sums, "batch", [(i, i ^ step) for i in range(batch)])
        step *= 2
    sums = sums[:, :7].T
    grad_values = grad_values.reshape(values.shape)
    return mixed, grad_values, grad_gates, grad_spectrum.transpose(0, 2, 1), sums[0:3], sums[3:6], sums[6]


def solution(mesh):
    in_specs = (
        P(None, ("batch", "seq")),
        P(None, ("batch", "seq")),
        P(None, ("batch", "seq")),
        P(),
        P(),
        P(),
        P("batch", None),
        P(),
        P("seq", None, "batch"),
    )
    out_specs = (
        P(None, ("batch", "seq")),
        P(None, ("batch", "seq")),
        P(None, ("batch", "seq")),
        P("seq", None, "batch"),
        P(None, "seq"),
        P(None, "seq"),
        P("seq"),
    )
    return jax.shard_map(per_device, mesh=mesh, in_specs=in_specs, out_specs=out_specs, check_vma=False)
```

```python
import math

import jax
import jax.numpy as jnp
import numpy as np
from jax import lax
from jax.experimental import pallas as pl
from jax.experimental.pallas import tpu as pltpu
from jax.sharding import PartitionSpec as P


BLOCK = 1024
F32, BF16 = jnp.float32, jnp.bfloat16
GRANT = 20 << 20
PARTS, AHEAD = 4, 2


def cas_table():
    indices = np.arange(BLOCK, dtype=np.int32)
    products = indices[:, None] * indices[None, :] % BLOCK
    angles = products.astype(np.float32) * np.float32(2.0 * math.pi / BLOCK)
    table = (np.cos(angles) + np.sin(angles)) / np.float32(math.sqrt(BLOCK))
    return table.astype(jnp.bfloat16)


def lanes(shape=(32, 128)):
    return lax.broadcasted_iota(jnp.int32, shape, 1)


def back_in_time(now, before, steps, lane):
    return jnp.where(lane < steps, before, now)


def rolled(tile):
    return pltpu.roll(tile, 1, 1), pltpu.roll(tile, 2, 1)


def column(cols, at):
    return jnp.broadcast_to(cols[:, at : at + 1], (cols.shape[0], 128))


def gather_kernel(a_ref, b_ref, c_ref, out_ref, held, in_sems, out_sems):
    size = 32 // PARTS
    arrive, leave = [], []
    for p in range(PARTS):
        own = slice(p * size, p * size + size)
        arrive.append(
            [
                pltpu.make_async_copy(ref.at[own], held.at[own, k * 32 : k * 32 + 32, :], in_sems.at[p, k])
                for k, ref in enumerate((a_ref, b_ref, c_ref))
            ]
        )
        leave.append(pltpu.make_async_copy(held.at[own], out_ref.at[own], out_sems.at[p]))
    for part in arrive[:AHEAD]:
        for copy in part:
            copy.start()
    for p in range(PARTS):
        for one in arrive[p]:
            one.wait()
        leave[p].start()
        for one in arrive[p + AHEAD] if p + AHEAD < PARTS else ():
            one.start()
    for copy in leave:
        copy.wait()


def keep_kernel(table_ref, out_ref, sem):
    copy = pltpu.make_async_copy(table_ref, out_ref, sem)
    copy.start()
    copy.wait()


def shorten(tile, one, two, taps):
    return taps[0] * tile + taps[1] * one + taps[2] * two


def local_kernel(r_ref, cols_ref, lhs_ref):
    lane = lanes((16, 128))
    zero = jnp.zeros((16, 128), F32)
    for h in range(2):
        one, two, three = (slice(h * 16 + k * 32, h * 16 + k * 32 + 16) for k in range(3))
        cols = cols_ref[one, :]
        tv = [column(cols, k) for k in range(3)]
        tg = [column(cols, 3 + k) for k in range(3)]

        def block(i, carry):
            v1, v2, g1, g2 = carry
            rows = pl.multiple_of(i * 32, 32) + h * 16
            for t in range(8):
                piece, at = i * 4 + t // 2, slice((t % 2) * 128, (t % 2) * 128 + 128)
                v = r_ref[piece, one, at].astype(F32)
                g = r_ref[piece, two, at].astype(F32)
                c = r_ref[piece, three, at].astype(F32)
                nv1, nv2 = rolled(v)
                ng1, ng2 = rolled(g)
                short_v = shorten(v, back_in_time(nv1, v1, 1, lane), back_in_time(nv2, v2, 2, lane), tv)
                short_g = shorten(g, back_in_time(ng1, g1, 1, lane), back_in_time(ng2, g2, 2, lane), tg)
                lhs_ref[pl.ds(rows, 16), t * 128 : t * 128 + 128] = short_v.astype(BF16)
                lhs_ref[pl.ds(rows + 256, 16), t * 128 : t * 128 + 128] = (c * short_g).astype(BF16)
                v1, v2, g1, g2 = nv1, nv2, ng1, ng2
            return v1, v2, g1, g2

        lax.fori_loop(0, 8, block, (zero,) * 4)


def spread_kernel(part_ref, r_ref, rim_ref, cols_ref, tw_ref, cas_ref, out_ref, lhs):
    lane = lanes((16, 128))
    lhs[...] = part_ref[...]
    for h in range(2):
        one, two, three = (slice(h * 16 + k * 32, h * 16 + k * 32 + 16) for k in range(3))
        cols = cols_ref[one, :]
        short = []
        for k, own in enumerate((one, two)):
            tile = r_ref[0, own, 0:128].astype(F32)
            before = rolled(rim_ref[own, :].astype(F32))
            shifted = [back_in_time(a, b, n + 1, lane) for n, (a, b) in enumerate(zip(rolled(tile), before))]
            short.append(shorten(tile, *shifted, [column(cols, 3 * k + n) for n in range(3)]))
        lhs[one, 0:128] = short[0].astype(BF16)
        lhs[256 + h * 16 : 272 + h * 16, 0:128] = (r_ref[0, three, 0:128].astype(F32) * short[1]).astype(BF16)

    low = lanes((16, 128)) < 64

    def strip(n, _):
        at = pl.multiple_of(n * 256, 256)
        sums = jnp.dot(lhs[...], cas_ref[:, pl.ds(at, 256)], preferred_element_type=F32)
        for h in range(2):
            tw = tw_ref[:, pl.ds(pl.multiple_of(at + h * 128, 128), 128)]
            d = 4 * n + 2 * h
            for m in range(16):
                part = sums[m * 32 : m * 32 + 32, h * 128 : h * 128 + 128] * tw[m % 8 : m % 8 + 1, :]
                a, b = part[:16], part[16:]
                even = jnp.where(low, a, pltpu.roll(b, 64, 1))
                odd = jnp.where(low, pltpu.roll(a, 64, 1), b)
                out_ref[d, m * 16 : m * 16 + 16, :] = even.astype(BF16)
                out_ref[d + 1, m * 16 : m * 16 + 16, :] = odd.astype(BF16)
        return 0

    lax.fori_loop(0, 4, strip, 0)


def mix_kernel(f_ref, spec_ref, mix_ref, gs_ref, out_ref, wide_v, wide_g, stage, sems):
    wide = (wide_v, wide_g)
    for f in range(2):
        for b in range(16):
            wide[f][b * 128 : b * 128 + 128, :] = f_ref[b, f * 128 : f * 128 + 128, :].astype(F32)
    mixing = mix_ref[...]
    turned = mixing.T
    high = turned.astype(BF16)
    low = (turned - high.astype(F32)).astype(BF16)
    ahead = jnp.concatenate([high, low], axis=1)
    again = jnp.concatenate([jnp.concatenate([high, high], axis=1), jnp.concatenate([low, low], axis=1)], axis=0)

    leaving = []
    for c in range(16):
        slabs = [wide[f][pl.ds(c, 128, stride=16), :].T.astype(BF16) for f in range(2)]
        both = jnp.dot(jnp.concatenate(slabs, axis=0), ahead, preferred_element_type=F32)
        both = both[:, :128] + both[:, 128:]
        sv, sg = both[:128], both[128:]
        filters = jnp.concatenate([spec_ref[c], spec_ref[16 + c]], axis=0).astype(F32)
        grad = sv * sg
        for n, channel in enumerate((c, 16 + c)):
            stage[channel] = grad[n * 64 : n * 64 + 64]
            leaving.append(pltpu.make_async_copy(stage.at[channel], gs_ref.at[channel], sems.at[channel]))
            leaving[-1].start()
        product = jnp.concatenate([sv * filters, sg * filters], axis=0)
        top = product.astype(BF16)
        rest = (product - top.astype(F32)).astype(BF16)
        product = jnp.concatenate([top, rest], axis=1)
        sums = lax.dot_general(again, product, (((1,), (1,)), ((), ())), preferred_element_type=F32)
        sums = sums[:128] + sums[128:]
        for f in range(2):
            wide[f][pl.ds(c, 128, stride=16), :] = sums[:, f * 128 : f * 128 + 128]
    for f in range(2):
        for b in range(16):
            out_ref[b, f * 128 : f * 128 + 128, :] = wide[f][b * 128 : b * 128 + 128, :].astype(BF16)
    for copy in leaving:
        copy.wait()


def back_kernel(y_ref, r_ref, rim_ref, cols_ref, tw_ref, cas_ref, out_ref, head_ref, lhs):
    low = lanes((16, 128)) < 64

    def unpack(y, _):
        at = pl.multiple_of(y * 128, 128)
        tw = tw_ref[:, pl.ds(at, 128)]
        for m in range(16):
            e = y_ref[2 * y, m * 16 : m * 16 + 16, :].astype(F32)
            o = y_ref[2 * y + 1, m * 16 : m * 16 + 16, :].astype(F32)
            row = tw[m % 8 : m % 8 + 1, :]
            a = jnp.where(low, e, pltpu.roll(o, 64, 1)) * row
            b = jnp.where(low, pltpu.roll(e, 64, 1), o) * row
            lhs[m * 32 : m * 32 + 16, pl.ds(at, 128)] = a.astype(BF16)
            lhs[m * 32 + 16 : m * 32 + 32, pl.ds(at, 128)] = b.astype(BF16)
        return 0

    lax.fori_loop(0, 8, unpack, 0)

    def strip(n, _):
        at = pl.multiple_of(n * 256, 256)
        sums = jnp.dot(lhs[...], cas_ref[:, pl.ds(at, 256)], preferred_element_type=F32)
        out_ref[:, pl.ds(at, 256)] = sums.astype(BF16)
        return 0

    lax.fori_loop(0, 4, strip, 0)

    lane = lanes()
    cols = cols_ref[...]
    v, g, c = (r_ref[0, k * 32 : k * 32 + 32, 0:128].astype(F32) for k in range(3))
    before_v, before_g = rim_ref[0:32, :].astype(F32), rim_ref[32:64, :].astype(F32)
    short_v, short_g = v * column(cols, 0), g * column(cols, 3)
    for k in (1, 2):
        short_v += column(cols, k) * back_in_time(pltpu.roll(v, k, 1), pltpu.roll(before_v, k, 1), k, lane)
        short_g += column(cols, 3 + k) * back_in_time(pltpu.roll(g, k, 1), pltpu.roll(before_g, k, 1), k, lane)
    short_v = short_v.astype(BF16).astype(F32)
    grad_long = (c * short_g).astype(BF16).astype(F32)
    skip = column(cols, 6)
    head_ref[0:32, :] = skip * grad_long + out_ref[256:288, 0:128].astype(F32)
    head_ref[32:64, :] = c * (out_ref[0:32, 0:128].astype(F32) + skip * short_v)


def finish(r_ref, d_ref, rim_ref, cols_ref, stage, heads, sums_ref, first, count, following, on_block):
    lane = lanes((16, 128))

    def ahead(tile):
        return pltpu.roll(tile, 127, 1), pltpu.roll(tile, 126, 1)

    for h in range(2):
        one, two, three = (slice(h * 16 + k * 32, h * 16 + k * 32 + 16) for k in range(3))
        cols = cols_ref[one, :]
        tv = [column(cols, k) for k in range(3)]
        tg = [column(cols, 3 + k) for k in range(3)]
        skip = column(cols, 6)

        def gradients(v, vb, g, gb, c, long_v, back_g):
            short_v = shorten(v, *vb, tv).astype(BF16).astype(F32)
            short_g = shorten(g, *gb, tg)
            grad_long = (c * short_g).astype(BF16).astype(F32)
            direct = long_v + skip * short_v
            return short_v, short_g, grad_long, direct, skip * grad_long + back_g, c * direct

        def block(step, carry):
            i = first + count - 1 - step
            (v, v1, v2), (g, g1, g2), nv, acc = carry
            rows = pl.multiple_of(i * 32, 32) + h * 16
            for t in reversed(range(8)):
                piece, at = i * 4 + t // 2, slice((t % 2) * 128, (t % 2) * 128 + 128)
                if t > 0:
                    piece_b, at_b = i * 4 + (t - 1) // 2, slice(((t - 1) % 2) * 128, ((t - 1) % 2) * 128 + 128)
                    pv = r_ref[piece_b, one, at_b].astype(F32)
                    pg = r_ref[piece_b, two, at_b].astype(F32)
                else:
                    inside = i > 0
                    piece_b = jnp.maximum(i * 4 - 1, 0)
                    pv = jnp.where(inside, r_ref[piece_b, one, 128:256].astype(F32), rim_ref[one, :].astype(F32))
                    pg = jnp.where(inside, r_ref[piece_b, two, 128:256].astype(F32), rim_ref[two, :].astype(F32))
                pv1, pv2 = rolled(pv)
                pg1, pg2 = rolled(pg)
                vb = back_in_time(v1, pv1, 1, lane), back_in_time(v2, pv2, 2, lane)
                gb = back_in_time(g1, pg1, 1, lane), back_in_time(g2, pg2, 2, lane)
                c = r_ref[piece, three, at].astype(F32)
                long_v = d_ref[pl.ds(rows, 16), t * 128 : t * 128 + 128].astype(F32)
                back_g = d_ref[pl.ds(rows + 256, 16), t * 128 : t * 128 + 128].astype(F32)
                short_v, _, grad_long, direct, gsv, gsg = gradients(v, vb, g, gb, c, long_v, back_g)
                wv = ahead(gsv)
                put = piece - first * 4
                stage[put, one, at] = direct.astype(BF16)
                stage[put, two, at] = shorten(
                    gsv, jnp.where(lane > 126, nv[0], wv[0]), jnp.where(lane > 125, nv[1], wv[1]), tv
                ).astype(BF16)
                if t % 2 == 0:
                    heads[pl.ds(pl.multiple_of(put * 32, 32) + h * 16, 16), :] = gsg.astype(BF16)
                terms = (gsv * v, gsv * vb[0], gsv * vb[1], gsg * g, gsg * gb[0], gsg * gb[1], grad_long * short_v)
                acc = tuple(a + b for a, b in zip(acc, terms))
                v, v1, v2, g, g1, g2, nv = pv, pv1, pv2, pg, pg1, pg2, wv
            if h == 1:
                on_block(i - first)
            return (v, v1, v2), (g, g1, g2), nv, acc

        end = first * 4 + count * 4 - 1
        last_v = r_ref[end, one, 128:256].astype(F32)
        last_g = r_ref[end, two, 128:256].astype(F32)
        last_v = last_v, *rolled(last_v)
        last_g = last_g, *rolled(last_g)
        if following is None:
            rows = (first + count) * 32 + h * 16
            next_v, next_g, c = (r_ref[end + 1, own, 0:128].astype(F32) for own in (one, two, three))
            vb = [back_in_time(a, b, n + 1, lane) for n, (a, b) in enumerate(zip(rolled(next_v), last_v[1:]))]
            gb = [back_in_time(a, b, n + 1, lane) for n, (a, b) in enumerate(zip(rolled(next_g), last_g[1:]))]
            long_v = d_ref[rows : rows + 16, 0:128].astype(F32)
            back_g = d_ref[rows + 256 : rows + 272, 0:128].astype(F32)
            gsv = gradients(next_v, vb, next_g, gb, c, long_v, back_g)[4]
        else:
            gsv = following[one, :]
        zero = jnp.zeros((16, 128), F32)
        start = last_v, last_g, ahead(gsv), (zero,) * 7
        acc = lax.fori_loop(0, count, block, start)[3]
        total = zero
        for k in range(7):
            total = jnp.where(lane == k, jnp.sum(acc[k], axis=1, keepdims=True), total)
        sums_ref[one, :] = total


def most_kernel(d_ref, r_ref, rim_ref, cols_ref, out_ref, sums_ref, heads_ref, stage, sems):
    def leave(i):
        own = pl.ds(i * 4, 4)
        return pltpu.make_async_copy(stage.at[own], out_ref.at[own, 0:64, :], sems.at[i])

    def on_block(i):
        leave(i).start()

    finish(r_ref, d_ref, rim_ref, cols_ref, stage, heads_ref, sums_ref, 0, 7, None, on_block)
    for i in range(7):
        leave(i).wait()


def last_kernel(
    most_ref, d_ref, r_ref, rim_ref, next_ref, cols_ref, some_ref, heads_ref, out_ref, sums_ref, stage, edges, held, sems
):
    finish(r_ref, d_ref, rim_ref, cols_ref, stage, held, sums_ref, 7, 1, next_ref, lambda i: None)
    copies = [
        pltpu.make_async_copy(stage, out_ref.at[28:32, 0:64, :], sems.at[0]),
        pltpu.make_async_copy(edges, out_ref.at[:, 64:72, :], sems.at[1]),
    ]
    copies[0].start()
    sums_ref[...] = sums_ref[...] + some_ref[...]
    held[128:160, :] = next_ref[32:64, :].astype(BF16)
    line = lax.broadcasted_iota(jnp.int32, (8, 128), 0)
    lane = lanes((8, 128))
    after = ((line < 2) & (lane == line)).astype(F32).astype(BF16)
    before = ((line > 1) & (line < 4) & (lane == line + 124)).astype(F32).astype(BF16)
    dims = (((1,), (1,)), ((), ()))
    edges[:, :, 128:256] = jnp.zeros((32, 8, 128), BF16)
    for j in range(8):
        if j < 6:
            ahead = heads_ref[j * 128 + 32 : j * 128 + 160, :]
        elif j == 6:
            ahead = jnp.concatenate([heads_ref[800:896, :], held[0:32, :]], axis=0)
        else:
            ahead = held[32:160, :]
        pieces = [r_ref[p, 32:64, 128:256] if p >= 0 else rim_ref[32:64, :] for p in range(4 * j - 1, 4 * j + 3)]
        rows = lax.dot_general(after, ahead, dims, preferred_element_type=F32)
        rows += lax.dot_general(before, jnp.concatenate(pieces, axis=0), dims, preferred_element_type=F32)
        for p in range(4 * j, 4 * j + 4):
            edges[p, :, 0:128] = rows.astype(BF16)
    copies[1].start()
    for copy in copies:
        copy.wait()


def home_kernel(
    u_ref, g_ref, c_ref, cols_ref, sel_ref, mixed_ref, gv_ref, gg_ref, stage_m, stage_g, turned, sems
):
    direct = pltpu.make_async_copy(u_ref.at[:, 32:64, :], gv_ref, sems.at[0, 2])
    direct.start()
    lane = lanes((16, 128))
    for j in range(4):
        edge = u_ref[j * 8 : j * 8 + 8, 64:72, 0:128].astype(F32).reshape(64, 128).astype(BF16)
        turned[j] = lax.dot_general(sel_ref[...], edge, (((1,), (1,)), ((), ())), preferred_element_type=F32)

    def leave(j):
        own = pl.ds(pl.multiple_of(j * 256, 256), 256)
        return (
            pltpu.make_async_copy(stage_m.at[own], mixed_ref.at[own], sems.at[j, 0]),
            pltpu.make_async_copy(stage_g.at[own], gg_ref.at[own], sems.at[j, 1]),
        )

    def part(j, _):
        for k in range(8):
            for h in range(2):
                q = j * 8 + k
                rows = pl.ds(pl.multiple_of(q * 32, 32) + h * 16, 16)
                own = slice(h * 16, h * 16 + 16)
                after0, after1, before2, before1 = (
                    jnp.broadcast_to(turned[j, own, k * 8 + n : k * 8 + n + 1], (16, 128)) for n in range(4)
                )
                cols = cols_ref[rows, :]
                tg = [column(cols, n) for n in range(3)]
                g, c, u = (
                    [ref[:, at : at + 128].astype(F32) for at in (0, 128)]
                    for ref in (g_ref.at[rows], c_ref.at[rows], u_ref.at[q, own])
                )
                ones, twos = zip(*(rolled(x) for x in g))
                one = jnp.where(lane < 1, before1, ones[0]), back_in_time(ones[1], ones[0], 1, lane)
                two = jnp.where(lane < 1, before2, back_in_time(twos[0], before1, 2, lane)), back_in_time(twos[1], twos[0], 2, lane)
                s = [a * b for a, b in zip(c, u)]
                left = [(pltpu.roll(x, 127, 1), pltpu.roll(x, 126, 1)) for x in s]
                next1 = jnp.where(lane > 126, left[1][0], left[0][0]), jnp.where(lane > 126, after0, left[1][0])
                next2 = (
                    jnp.where(lane > 125, left[1][1], left[0][1]),
                    jnp.where(lane > 126, after1, jnp.where(lane > 125, after0, left[1][1])),
                )
                for n, at in enumerate((0, 128)):
                    stage_m[rows, at : at + 128] = (shorten(g[n], one[n], two[n], tg) * u[n]).astype(BF16)
                    stage_g[rows, at : at + 128] = shorten(s[n], next1[n], next2[n], tg).astype(BF16)
        for copy in leave(j):
            copy.start()
        return 0

    lax.fori_loop(0, 4, part, 0)
    direct.wait()
    for j in range(4):
        for copy in leave(j):
            copy.wait()


VMEM = pl.BlockSpec(memory_space=pltpu.VMEM)
ANY = pl.BlockSpec(memory_space=pl.ANY)


def call(kernel, outs, scratch, flops, moved, *args, **more):
    return pl.pallas_call(
        kernel,
        **{"in_specs": [VMEM] * len(args), "out_specs": [VMEM] * len(outs), **more},
        compiler_params=pltpu.CompilerParams(vmem_limit_bytes=GRANT),
        out_shape=[jax.ShapeDtypeStruct(s, d) for s, d in outs],
        scratch_shapes=[s if d is None else pltpu.VMEM(s, d) for s, d in scratch],
        cost_estimate=pl.CostEstimate(flops=flops, bytes_accessed=moved, transcendentals=0),
    )(*args)


def local(r, cols):
    return call(local_kernel, [((512, 1024), BF16)], [], 1 << 24, 4 << 20, r, cols)[0]


def spread(part, r, rim, cols, twiddle, cas):
    return call(
        spread_kernel,
        [((16, 256, 128), BF16)],
        [((512, 1024), BF16)],
        1 << 30,
        5 << 20,
        part,
        r,
        rim,
        cols,
        twiddle,
        cas,
    )[0]


def mix(by_freq, spectrum, mixing):
    return call(
        mix_kernel,
        [((32, 64, 128), F32), ((16, 256, 128), BF16)],
        [
            ((2048, 128), F32),
            ((2048, 128), F32),
            ((32, 64, 128), F32),
            (pltpu.SemaphoreType.DMA((32,)), None),
        ],
        1 << 30,
        5 << 20,
        by_freq,
        spectrum,
        mixing,
        out_specs=[ANY, VMEM],
    )


def back(returned, r, rim, cols, twiddle, cas):
    return call(
        back_kernel,
        [((512, 1024), BF16), ((64, 128), F32)],
        [((512, 1024), BF16)],
        1 << 30,
        5 << 20,
        returned,
        r,
        rim,
        cols,
        twiddle,
        cas,
    )


def most(d, r, rim, cols):
    return call(
        most_kernel,
        [((32, 72, 256), BF16), ((32, 128), F32), ((896, 128), BF16)],
        [((28, 64, 256), BF16), (pltpu.SemaphoreType.DMA((7,)), None)],
        1 << 25,
        8 << 20,
        d,
        r,
        rim,
        cols,
        out_specs=[ANY, VMEM, VMEM],
    )


def last(done, d, r, rim, following, cols, sums, heads):
    return call(
        last_kernel,
        [((32, 72, 256), BF16), ((32, 128), F32)],
        [
            ((4, 64, 256), BF16),
            ((32, 8, 256), BF16),
            ((160, 128), BF16),
            (pltpu.SemaphoreType.DMA((2,)), None),
        ],
        1 << 22,
        1 << 20,
        done,
        d,
        r,
        rim,
        following,
        cols,
        sums,
        heads,
        in_specs=[ANY] + [VMEM] * 7,
        out_specs=[ANY, VMEM],
        input_output_aliases={0: 0},
    )


def home(u, gates, cotangent, cols, sel):
    return call(
        home_kernel,
        [((1024, 256), BF16), ((32, 32, 256), BF16), ((1024, 256), BF16)],
        [
            ((1024, 256), BF16),
            ((1024, 256), BF16),
            ((4, 32, 64), F32),
            (pltpu.SemaphoreType.DMA((4, 3)), None),
        ],
        1 << 24,
        6 << 20,
        u,
        gates,
        cotangent,
        cols,
        sel,
        out_specs=[ANY] * 3,
    )


def gather(*fields):
    return pl.pallas_call(
        gather_kernel,
        in_specs=[pl.BlockSpec(memory_space=pl.ANY)] * 3,
        out_specs=pl.BlockSpec(memory_space=pl.ANY),
        out_shape=jax.ShapeDtypeStruct((32, 96, 256), BF16),
        scratch_shapes=[
            pltpu.VMEM((32, 96, 256), BF16),
            pltpu.SemaphoreType.DMA((PARTS, 3)),
            pltpu.SemaphoreType.DMA((PARTS,)),
        ],
    )(*fields)


def keep(table):
    return pl.pallas_call(
        keep_kernel,
        in_specs=[pl.BlockSpec(memory_space=pl.ANY)],
        out_specs=pl.BlockSpec(memory_space=pltpu.VMEM),
        out_shape=jax.ShapeDtypeStruct(table.shape, table.dtype),
        scratch_shapes=[pltpu.SemaphoreType.DMA(())],
        compiler_params=pltpu.CompilerParams(vmem_limit_bytes=GRANT),
        cost_estimate=pl.CostEstimate(flops=0, bytes_accessed=4 << 20, transcendentals=0),
    )(table)


def exchange(array, axis):
    return lax.all_to_all(array, axis, 0, 0, tiled=True)


def per_device(values, gates, cotangent, taps_values, taps_gates, skip_gain, twiddle, mixing, spectrum):
    batch = lax.axis_size("batch")
    raw = gather(*(x.reshape(32, 32, 256) for x in (values, gates, cotangent)))
    r = exchange(raw, "seq")
    cas = keep(jnp.asarray(cas_table()))
    gains = jnp.concatenate([taps_values, taps_gates, skip_gain[None]], axis=0)
    cols = lax.dynamic_slice(gains, (0, lax.axis_index("seq") * 32), (7, 32))
    cols = jnp.pad(cols.T, ((0, 0), (0, 121)))
    rim = lax.ppermute(r[31, :64, 128:], "batch", [(i, i + 1) for i in range(batch - 1)])
    by_freq = exchange(spread(local(r, cols), r, rim, cols, twiddle, cas), "batch")
    grad_spectrum, weighted = mix(by_freq, spectrum.transpose(0, 2, 1), mixing)
    d, head = back(exchange(weighted, "batch"), r, rim, cols, twiddle, cas)
    following = lax.ppermute(head, "batch", [(i + 1, i) for i in range(batch - 1)])
    done, sums, heads = most(d, r, rim, cols)
    done, sums = last(done, d, r, rim, following, cols, sums, heads)
    outs = exchange(done, "seq")
    gate_cols = jnp.pad(taps_gates.T, ((0, 0), (0, 125)))
    own = lax.rem(lax.axis_index("seq"), 4) * 32 + lax.broadcasted_iota(jnp.int32, (32, 128), 0)
    sel = (own == lanes()).astype(BF16)
    mixed, grad_values, grad_gates = home(outs, gates, cotangent, gate_cols, sel)
    step = 1
    while step < batch:
        sums = sums + lax.ppermute(sums, "batch", [(i, i ^ step) for i in range(batch)])
        step *= 2
    sums = sums[:, :7].T
    grad_values = grad_values.reshape(values.shape)
    return mixed, grad_values, grad_gates, grad_spectrum.transpose(0, 2, 1), sums[0:3], sums[3:6], sums[6]


def solution(mesh):
    in_specs = (
        P(None, ("batch", "seq")),
        P(None, ("batch", "seq")),
        P(None, ("batch", "seq")),
        P(),
        P(),
        P(),
        P("batch", None),
        P(),
        P("seq", None, "batch"),
    )
    out_specs = (
        P(None, ("batch", "seq")),
        P(None, ("batch", "seq")),
        P(None, ("batch", "seq")),
        P("seq", None, "batch"),
        P(None, "seq"),
        P(None, "seq"),
        P("seq"),
    )
    return jax.shard_map(per_device, mesh=mesh, in_specs=in_specs, out_specs=out_specs, check_vma=False)
```

```python
import math

import jax
import jax.numpy as jnp
import numpy as np
from jax import lax
from jax.experimental import pallas as pl
from jax.experimental.pallas import tpu as pltpu
from jax.sharding import PartitionSpec as P


BLOCK = 1024
F32, BF16 = jnp.float32, jnp.bfloat16
GRANT = 20 << 20
PARTS = 8


def cas_table():
    indices = np.arange(BLOCK, dtype=np.int32)
    products = indices[:, None] * indices[None, :] % BLOCK
    angles = products.astype(np.float32) * np.float32(2.0 * math.pi / BLOCK)
    table = (np.cos(angles) + np.sin(angles)) / np.float32(math.sqrt(BLOCK))
    return table.astype(jnp.bfloat16)


def lanes(shape=(32, 128)):
    return lax.broadcasted_iota(jnp.int32, shape, 1)


def back_in_time(now, before, steps, lane):
    return jnp.where(lane < steps, before, now)


def rolled(tile):
    return pltpu.roll(tile, 1, 1), pltpu.roll(tile, 2, 1)


def column(cols, at):
    return jnp.broadcast_to(cols[:, at : at + 1], (cols.shape[0], 128))


def gather_kernel(a_ref, b_ref, c_ref, out_ref, held, in_sems, out_sems):
    size = 32 // PARTS
    arrive, leave = [], []
    for p in range(PARTS):
        own = slice(p * size, p * size + size)
        arrive.append(
            [
                pltpu.make_async_copy(ref.at[own], held.at[own, k * 32 : k * 32 + 32, :], in_sems.at[p, k])
                for k, ref in enumerate((a_ref, b_ref, c_ref))
            ]
        )
        leave.append(pltpu.make_async_copy(held.at[own], out_ref.at[own], out_sems.at[p]))
    for part in arrive:
        for copy in part:
            copy.start()
    for part, copy in zip(arrive, leave):
        for one in part:
            one.wait()
        copy.start()
    for copy in leave:
        copy.wait()


def keep_kernel(table_ref, out_ref, sem):
    copy = pltpu.make_async_copy(table_ref, out_ref, sem)
    copy.start()
    copy.wait()


def shorten(tile, one, two, taps):
    return taps[0] * tile + taps[1] * one + taps[2] * two


def local_kernel(r_ref, cols_ref, lhs_ref):
    lane = lanes((16, 128))
    zero = jnp.zeros((16, 128), F32)
    for h in range(2):
        one, two, three = (slice(h * 16 + k * 32, h * 16 + k * 32 + 16) for k in range(3))
        cols = cols_ref[one, :]
        tv = [column(cols, k) for k in range(3)]
        tg = [column(cols, 3 + k) for k in range(3)]

        def block(i, carry):
            v1, v2, g1, g2 = carry
            rows = pl.multiple_of(i * 32, 32) + h * 16
            for t in range(8):
                piece, at = i * 4 + t // 2, slice((t % 2) * 128, (t % 2) * 128 + 128)
                v = r_ref[piece, one, at].astype(F32)
                g = r_ref[piece, two, at].astype(F32)
                c = r_ref[piece, three, at].astype(F32)
                nv1, nv2 = rolled(v)
                ng1, ng2 = rolled(g)
                short_v = shorten(v, back_in_time(nv1, v1, 1, lane), back_in_time(nv2, v2, 2, lane), tv)
                short_g = shorten(g, back_in_time(ng1, g1, 1, lane), back_in_time(ng2, g2, 2, lane), tg)
                lhs_ref[pl.ds(rows, 16), t * 128 : t * 128 + 128] = short_v.astype(BF16)
                lhs_ref[pl.ds(rows + 256, 16), t * 128 : t * 128 + 128] = (c * short_g).astype(BF16)
                v1, v2, g1, g2 = nv1, nv2, ng1, ng2
            return v1, v2, g1, g2

        lax.fori_loop(0, 8, block, (zero,) * 4)


def spread_kernel(part_ref, r_ref, rim_ref, cols_ref, tw_ref, cas_ref, out_ref, lhs):
    lane = lanes((16, 128))
    lhs[...] = part_ref[...]
    for h in range(2):
        one, two, three = (slice(h * 16 + k * 32, h * 16 + k * 32 + 16) for k in range(3))
        cols = cols_ref[one, :]
        short = []
        for k, own in enumerate((one, two)):
            tile = r_ref[0, own, 0:128].astype(F32)
            before = rolled(rim_ref[own, :].astype(F32))
            shifted = [back_in_time(a, b, n + 1, lane) for n, (a, b) in enumerate(zip(rolled(tile), before))]
            short.append(shorten(tile, *shifted, [column(cols, 3 * k + n) for n in range(3)]))
        lhs[one, 0:128] = short[0].astype(BF16)
        lhs[256 + h * 16 : 272 + h * 16, 0:128] = (r_ref[0, three, 0:128].astype(F32) * short[1]).astype(BF16)

    low = lanes((16, 128)) < 64

    def strip(n, _):
        at = pl.multiple_of(n * 256, 256)
        sums = jnp.dot(lhs[...], cas_ref[:, pl.ds(at, 256)], preferred_element_type=F32)
        for h in range(2):
            tw = tw_ref[:, pl.ds(pl.multiple_of(at + h * 128, 128), 128)]
            d = 4 * n + 2 * h
            for m in range(16):
                part = sums[m * 32 : m * 32 + 32, h * 128 : h * 128 + 128] * tw[m % 8 : m % 8 + 1, :]
                a, b = part[:16], part[16:]
                even = jnp.where(low, a, pltpu.roll(b, 64, 1))
                odd = jnp.where(low, pltpu.roll(a, 64, 1), b)
                out_ref[d, m * 16 : m * 16 + 16, :] = even.astype(BF16)
                out_ref[d + 1, m * 16 : m * 16 + 16, :] = odd.astype(BF16)
        return 0

    lax.fori_loop(0, 4, strip, 0)


def mix_kernel(f_ref, spec_ref, mix_ref, gs_ref, out_ref, wide_v, wide_g):
    wide = (wide_v, wide_g)
    for f in range(2):
        for b in range(16):
            wide[f][b * 128 : b * 128 + 128, :] = f_ref[b, f * 128 : f * 128 + 128, :].astype(F32)
    mixing = mix_ref[...]
    turned = mixing.T
    high = turned.astype(BF16)
    low = (turned - high.astype(F32)).astype(BF16)
    ahead = jnp.concatenate([high, low], axis=1)
    again = jnp.concatenate([jnp.concatenate([high, high], axis=1), jnp.concatenate([low, low], axis=1)], axis=0)

    for c in range(16):
        slabs = [wide[f][pl.ds(c, 128, stride=16), :].T.astype(BF16) for f in range(2)]
        both = jnp.dot(jnp.concatenate(slabs, axis=0), ahead, preferred_element_type=F32)
        both = both[:, :128] + both[:, 128:]
        sv, sg = both[:128], both[128:]
        filters = jnp.concatenate([spec_ref[c], spec_ref[16 + c]], axis=0).astype(F32)
        grad = sv * sg
        gs_ref[c] = grad[:64]
        gs_ref[16 + c] = grad[64:]
        product = jnp.concatenate([sv * filters, sg * filters], axis=0)
        top = product.astype(BF16)
        rest = (product - top.astype(F32)).astype(BF16)
        product = jnp.concatenate([top, rest], axis=1)
        sums = lax.dot_general(again, product, (((1,), (1,)), ((), ())), preferred_element_type=F32)
        sums = sums[:128] + sums[128:]
        for f in range(2):
            wide[f][pl.ds(c, 128, stride=16), :] = sums[:, f * 128 : f * 128 + 128]
    for f in range(2):
        for b in range(16):
            out_ref[b, f * 128 : f * 128 + 128, :] = wide[f][b * 128 : b * 128 + 128, :].astype(BF16)


def back_kernel(y_ref, r_ref, rim_ref, cols_ref, tw_ref, cas_ref, out_ref, head_ref, lhs):
    low = lanes((16, 128)) < 64

    def unpack(y, _):
        at = pl.multiple_of(y * 128, 128)
        tw = tw_ref[:, pl.ds(at, 128)]
        for m in range(16):
            e = y_ref[2 * y, m * 16 : m * 16 + 16, :].astype(F32)
            o = y_ref[2 * y + 1, m * 16 : m * 16 + 16, :].astype(F32)
            row = tw[m % 8 : m % 8 + 1, :]
            a = jnp.where(low, e, pltpu.roll(o, 64, 1)) * row
            b = jnp.where(low, pltpu.roll(e, 64, 1), o) * row
            lhs[m * 32 : m * 32 + 16, pl.ds(at, 128)] = a.astype(BF16)
            lhs[m * 32 + 16 : m * 32 + 32, pl.ds(at, 128)] = b.astype(BF16)
        return 0

    lax.fori_loop(0, 8, unpack, 0)

    def strip(n, _):
        at = pl.multiple_of(n * 256, 256)
        sums = jnp.dot(lhs[...], cas_ref[:, pl.ds(at, 256)], preferred_element_type=F32)
        out_ref[:, pl.ds(at, 256)] = sums.astype(BF16)
        return 0

    lax.fori_loop(0, 4, strip, 0)

    lane = lanes()
    cols = cols_ref[...]
    v, g, c = (r_ref[0, k * 32 : k * 32 + 32, 0:128].astype(F32) for k in range(3))
    before_v, before_g = rim_ref[0:32, :].astype(F32), rim_ref[32:64, :].astype(F32)
    short_v, short_g = v * column(cols, 0), g * column(cols, 3)
    for k in (1, 2):
        short_v += column(cols, k) * back_in_time(pltpu.roll(v, k, 1), pltpu.roll(before_v, k, 1), k, lane)
        short_g += column(cols, 3 + k) * back_in_time(pltpu.roll(g, k, 1), pltpu.roll(before_g, k, 1), k, lane)
    short_v = short_v.astype(BF16).astype(F32)
    grad_long = (c * short_g).astype(BF16).astype(F32)
    skip = column(cols, 6)
    head_ref[0:32, :] = skip * grad_long + out_ref[256:288, 0:128].astype(F32)
    head_ref[32:64, :] = c * (out_ref[0:32, 0:128].astype(F32) + skip * short_v)


def finish(r_ref, d_ref, rim_ref, cols_ref, stage, heads, sums_ref, first, count, following, on_block):
    lane = lanes((16, 128))

    def ahead(tile):
        return pltpu.roll(tile, 127, 1), pltpu.roll(tile, 126, 1)

    for h in range(2):
        one, two, three = (slice(h * 16 + k * 32, h * 16 + k * 32 + 16) for k in range(3))
        cols = cols_ref[one, :]
        tv = [column(cols, k) for k in range(3)]
        tg = [column(cols, 3 + k) for k in range(3)]
        skip = column(cols, 6)

        def gradients(v, vb, g, gb, c, long_v, back_g):
            short_v = shorten(v, *vb, tv).astype(BF16).astype(F32)
            short_g = shorten(g, *gb, tg)
            grad_long = (c * short_g).astype(BF16).astype(F32)
            direct = long_v + skip * short_v
            return short_v, short_g, grad_long, direct, skip * grad_long + back_g, c * direct

        def block(step, carry):
            i = first + count - 1 - step
            (v, v1, v2), (g, g1, g2), nv, acc = carry
            rows = pl.multiple_of(i * 32, 32) + h * 16
            for t in reversed(range(8)):
                piece, at = i * 4 + t // 2, slice((t % 2) * 128, (t % 2) * 128 + 128)
                if t > 0:
                    piece_b, at_b = i * 4 + (t - 1) // 2, slice(((t - 1) % 2) * 128, ((t - 1) % 2) * 128 + 128)
                    pv = r_ref[piece_b, one, at_b].astype(F32)
                    pg = r_ref[piece_b, two, at_b].astype(F32)
                else:
                    inside = i > 0
                    piece_b = jnp.maximum(i * 4 - 1, 0)
                    pv = jnp.where(inside, r_ref[piece_b, one, 128:256].astype(F32), rim_ref[one, :].astype(F32))
                    pg = jnp.where(inside, r_ref[piece_b, two, 128:256].astype(F32), rim_ref[two, :].astype(F32))
                pv1, pv2 = rolled(pv)
                pg1, pg2 = rolled(pg)
                vb = back_in_time(v1, pv1, 1, lane), back_in_time(v2, pv2, 2, lane)
                gb = back_in_time(g1, pg1, 1, lane), back_in_time(g2, pg2, 2, lane)
                c = r_ref[piece, three, at].astype(F32)
                long_v = d_ref[pl.ds(rows, 16), t * 128 : t * 128 + 128].astype(F32)
                back_g = d_ref[pl.ds(rows + 256, 16), t * 128 : t * 128 + 128].astype(F32)
                short_v, _, grad_long, direct, gsv, gsg = gradients(v, vb, g, gb, c, long_v, back_g)
                wv = ahead(gsv)
                put = piece - first * 4
                stage[put, one, at] = direct.astype(BF16)
                stage[put, two, at] = shorten(
                    gsv, jnp.where(lane > 126, nv[0], wv[0]), jnp.where(lane > 125, nv[1], wv[1]), tv
                ).astype(BF16)
                if t % 2 == 0:
                    heads[pl.ds(pl.multiple_of(put * 32, 32) + h * 16, 16), :] = gsg.astype(BF16)
                terms = (gsv * v, gsv * vb[0], gsv * vb[1], gsg * g, gsg * gb[0], gsg * gb[1], grad_long * short_v)
                acc = tuple(a + b for a, b in zip(acc, terms))
                v, v1, v2, g, g1, g2, nv = pv, pv1, pv2, pg, pg1, pg2, wv
            if h == 1:
                on_block(i - first)
            return (v, v1, v2), (g, g1, g2), nv, acc

        end = first * 4 + count * 4 - 1
        last_v = r_ref[end, one, 128:256].astype(F32)
        last_g = r_ref[end, two, 128:256].astype(F32)
        last_v = last_v, *rolled(last_v)
        last_g = last_g, *rolled(last_g)
        if following is None:
            rows = (first + count) * 32 + h * 16
            next_v, next_g, c = (r_ref[end + 1, own, 0:128].astype(F32) for own in (one, two, three))
            vb = [back_in_time(a, b, n + 1, lane) for n, (a, b) in enumerate(zip(rolled(next_v), last_v[1:]))]
            gb = [back_in_time(a, b, n + 1, lane) for n, (a, b) in enumerate(zip(rolled(next_g), last_g[1:]))]
            long_v = d_ref[rows : rows + 16, 0:128].astype(F32)
            back_g = d_ref[rows + 256 : rows + 272, 0:128].astype(F32)
            gsv = gradients(next_v, vb, next_g, gb, c, long_v, back_g)[4]
        else:
            gsv = following[one, :]
        zero = jnp.zeros((16, 128), F32)
        start = last_v, last_g, ahead(gsv), (zero,) * 7
        acc = lax.fori_loop(0, count, block, start)[3]
        total = zero
        for k in range(7):
            total = jnp.where(lane == k, jnp.sum(acc[k], axis=1, keepdims=True), total)
        sums_ref[one, :] = total


def most_kernel(d_ref, r_ref, rim_ref, cols_ref, out_ref, sums_ref, heads_ref, stage, sems):
    def leave(i):
        own = pl.ds(i * 4, 4)
        return pltpu.make_async_copy(stage.at[own], out_ref.at[own, 0:64, :], sems.at[i])

    def on_block(i):
        leave(i).start()

    finish(r_ref, d_ref, rim_ref, cols_ref, stage, heads_ref, sums_ref, 0, 7, None, on_block)
    for i in range(7):
        leave(i).wait()


def last_kernel(
    most_ref, d_ref, r_ref, rim_ref, next_ref, cols_ref, some_ref, heads_ref, out_ref, sums_ref, stage, edges, held, sems
):
    line = lax.broadcasted_iota(jnp.int32, (8, 128), 0)
    lane = lanes((8, 128))
    after = ((line < 2) & (lane == line)).astype(F32).astype(BF16)
    before = ((line > 1) & (line < 4) & (lane == line + 124)).astype(F32).astype(BF16)
    dims = (((1,), (1,)), ((), ()))

    def edge_rows(j, ahead):
        pieces = [r_ref[p, 32:64, 128:256] if p >= 0 else rim_ref[32:64, :] for p in range(4 * j - 1, 4 * j + 3)]
        rows = lax.dot_general(after, ahead, dims, preferred_element_type=F32)
        rows += lax.dot_general(before, jnp.concatenate(pieces, axis=0), dims, preferred_element_type=F32)
        for p in range(4 * j, 4 * j + 4):
            edges[p, :, 0:128] = rows.astype(BF16)

    edges[:, :, 128:256] = jnp.zeros((32, 8, 128), BF16)
    copies = [
        pltpu.make_async_copy(edges.at[0:24], out_ref.at[0:24, 64:72, :], sems.at[0]),
        pltpu.make_async_copy(stage, out_ref.at[28:32, 0:64, :], sems.at[1]),
        pltpu.make_async_copy(edges.at[24:32], out_ref.at[24:32, 64:72, :], sems.at[2]),
    ]
    for j in range(6):
        edge_rows(j, heads_ref[j * 128 + 32 : j * 128 + 160, :])
    copies[0].start()
    finish(r_ref, d_ref, rim_ref, cols_ref, stage, held, sums_ref, 7, 1, next_ref, lambda i: None)
    copies[1].start()
    held[128:160, :] = next_ref[32:64, :].astype(BF16)
    edge_rows(6, jnp.concatenate([heads_ref[800:896, :], held[0:32, :]], axis=0))
    edge_rows(7, held[32:160, :])
    copies[2].start()
    sums_ref[...] = sums_ref[...] + some_ref[...]
    for copy in copies:
        copy.wait()


def home_kernel(
    u_ref, g_ref, c_ref, cols_ref, sel_ref, mixed_ref, gv_ref, gg_ref, stage_m, stage_g, turned, sems
):
    direct = pltpu.make_async_copy(u_ref.at[:, 32:64, :], gv_ref, sems.at[0, 2])
    direct.start()
    lane = lanes((16, 128))
    for j in range(2):
        edge = u_ref[j * 16 : j * 16 + 16, 64:72, 0:128].astype(F32).reshape(128, 128).astype(BF16)
        turned[j] = lax.dot_general(sel_ref[...], edge, (((1,), (1,)), ((), ())), preferred_element_type=F32)

    def leave(j):
        own = pl.ds(pl.multiple_of(j * 512, 512), 512)
        return (
            pltpu.make_async_copy(stage_m.at[own], mixed_ref.at[own], sems.at[j, 0]),
            pltpu.make_async_copy(stage_g.at[own], gg_ref.at[own], sems.at[j, 1]),
        )

    def half(j, _):
        for k in range(16):
            for h in range(2):
                q = j * 16 + k
                rows = pl.ds(pl.multiple_of(q * 32, 32) + h * 16, 16)
                own = slice(h * 16, h * 16 + 16)
                after0, after1, before2, before1 = (
                    jnp.broadcast_to(turned[j, own, k * 8 + n : k * 8 + n + 1], (16, 128)) for n in range(4)
                )
                cols = cols_ref[rows, :]
                tg = [column(cols, n) for n in range(3)]
                g, c, u = (
                    [ref[:, at : at + 128].astype(F32) for at in (0, 128)]
                    for ref in (g_ref.at[rows], c_ref.at[rows], u_ref.at[q, own])
                )
                ones, twos = zip(*(rolled(x) for x in g))
                one = jnp.where(lane < 1, before1, ones[0]), back_in_time(ones[1], ones[0], 1, lane)
                two = jnp.where(lane < 1, before2, back_in_time(twos[0], before1, 2, lane)), back_in_time(twos[1], twos[0], 2, lane)
                s = [a * b for a, b in zip(c, u)]
                left = [(pltpu.roll(x, 127, 1), pltpu.roll(x, 126, 1)) for x in s]
                next1 = jnp.where(lane > 126, left[1][0], left[0][0]), jnp.where(lane > 126, after0, left[1][0])
                next2 = (
                    jnp.where(lane > 125, left[1][1], left[0][1]),
                    jnp.where(lane > 126, after1, jnp.where(lane > 125, after0, left[1][1])),
                )
                for n, at in enumerate((0, 128)):
                    stage_m[rows, at : at + 128] = (shorten(g[n], one[n], two[n], tg) * u[n]).astype(BF16)
                    stage_g[rows, at : at + 128] = shorten(s[n], next1[n], next2[n], tg).astype(BF16)
        for copy in leave(j):
            copy.start()
        return 0

    lax.fori_loop(0, 2, half, 0)
    direct.wait()
    for j in range(2):
        for copy in leave(j):
            copy.wait()


VMEM = pl.BlockSpec(memory_space=pltpu.VMEM)
ANY = pl.BlockSpec(memory_space=pl.ANY)


def call(kernel, outs, scratch, flops, moved, *args, **more):
    return pl.pallas_call(
        kernel,
        **{"in_specs": [VMEM] * len(args), "out_specs": [VMEM] * len(outs), **more},
        compiler_params=pltpu.CompilerParams(vmem_limit_bytes=GRANT),
        out_shape=[jax.ShapeDtypeStruct(s, d) for s, d in outs],
        scratch_shapes=[s if d is None else pltpu.VMEM(s, d) for s, d in scratch],
        cost_estimate=pl.CostEstimate(flops=flops, bytes_accessed=moved, transcendentals=0),
    )(*args)


def local(r, cols):
    return call(local_kernel, [((512, 1024), BF16)], [], 1 << 24, 4 << 20, r, cols)[0]


def spread(part, r, rim, cols, twiddle, cas):
    return call(
        spread_kernel,
        [((16, 256, 128), BF16)],
        [((512, 1024), BF16)],
        1 << 30,
        5 << 20,
        part,
        r,
        rim,
        cols,
        twiddle,
        cas,
    )[0]


def mix(by_freq, spectrum, mixing):
    return call(
        mix_kernel,
        [((32, 64, 128), F32), ((16, 256, 128), BF16)],
        [((2048, 128), F32), ((2048, 128), F32)],
        1 << 30,
        5 << 20,
        by_freq,
        spectrum,
        mixing,
    )


def back(returned, r, rim, cols, twiddle, cas):
    return call(
        back_kernel,
        [((512, 1024), BF16), ((64, 128), F32)],
        [((512, 1024), BF16)],
        1 << 30,
        5 << 20,
        returned,
        r,
        rim,
        cols,
        twiddle,
        cas,
    )


def most(d, r, rim, cols):
    return call(
        most_kernel,
        [((32, 72, 256), BF16), ((32, 128), F32), ((896, 128), BF16)],
        [((28, 64, 256), BF16), (pltpu.SemaphoreType.DMA((7,)), None)],
        1 << 25,
        8 << 20,
        d,
        r,
        rim,
        cols,
        out_specs=[ANY, VMEM, VMEM],
    )


def last(done, d, r, rim, following, cols, sums, heads):
    return call(
        last_kernel,
        [((32, 72, 256), BF16), ((32, 128), F32)],
        [
            ((4, 64, 256), BF16),
            ((32, 8, 256), BF16),
            ((160, 128), BF16),
            (pltpu.SemaphoreType.DMA((3,)), None),
        ],
        1 << 22,
        1 << 20,
        done,
        d,
        r,
        rim,
        following,
        cols,
        sums,
        heads,
        in_specs=[ANY] + [VMEM] * 7,
        out_specs=[ANY, VMEM],
        input_output_aliases={0: 0},
    )


def home(u, gates, cotangent, cols, sel):
    return call(
        home_kernel,
        [((1024, 256), BF16), ((32, 32, 256), BF16), ((1024, 256), BF16)],
        [
            ((1024, 256), BF16),
            ((1024, 256), BF16),
            ((2, 32, 128), F32),
            (pltpu.SemaphoreType.DMA((2, 3)), None),
        ],
        1 << 24,
        6 << 20,
        u,
        gates,
        cotangent,
        cols,
        sel,
        out_specs=[ANY] * 3,
    )


def gather(*fields):
    return pl.pallas_call(
        gather_kernel,
        in_specs=[pl.BlockSpec(memory_space=pl.ANY)] * 3,
        out_specs=pl.BlockSpec(memory_space=pl.ANY),
        out_shape=jax.ShapeDtypeStruct((32, 96, 256), BF16),
        scratch_shapes=[
            pltpu.VMEM((32, 96, 256), BF16),
            pltpu.SemaphoreType.DMA((PARTS, 3)),
            pltpu.SemaphoreType.DMA((PARTS,)),
        ],
    )(*fields)


def keep(table):
    return pl.pallas_call(
        keep_kernel,
        in_specs=[pl.BlockSpec(memory_space=pl.ANY)],
        out_specs=pl.BlockSpec(memory_space=pltpu.VMEM),
        out_shape=jax.ShapeDtypeStruct(table.shape, table.dtype),
        scratch_shapes=[pltpu.SemaphoreType.DMA(())],
        compiler_params=pltpu.CompilerParams(vmem_limit_bytes=GRANT),
        cost_estimate=pl.CostEstimate(flops=0, bytes_accessed=4 << 20, transcendentals=0),
    )(table)


def exchange(array, axis):
    return lax.all_to_all(array, axis, 0, 0, tiled=True)


def per_device(values, gates, cotangent, taps_values, taps_gates, skip_gain, twiddle, mixing, spectrum):
    batch = lax.axis_size("batch")
    raw = gather(*(x.reshape(32, 32, 256) for x in (values, gates, cotangent)))
    r = exchange(raw, "seq")
    cas = keep(jnp.asarray(cas_table()))
    gains = jnp.concatenate([taps_values, taps_gates, skip_gain[None]], axis=0)
    cols = lax.dynamic_slice(gains, (0, lax.axis_index("seq") * 32), (7, 32))
    cols = jnp.pad(cols.T, ((0, 0), (0, 121)))
    rim = lax.ppermute(r[31, :64, 128:], "batch", [(i, i + 1) for i in range(batch - 1)])
    by_freq = exchange(spread(local(r, cols), r, rim, cols, twiddle, cas), "batch")
    grad_spectrum, weighted = mix(by_freq, spectrum.transpose(0, 2, 1), mixing)
    d, head = back(exchange(weighted, "batch"), r, rim, cols, twiddle, cas)
    following = lax.ppermute(head, "batch", [(i + 1, i) for i in range(batch - 1)])
    done, sums, heads = most(d, r, rim, cols)
    done, sums = last(done, d, r, rim, following, cols, sums, heads)
    outs = exchange(done, "seq")
    gate_cols = jnp.pad(taps_gates.T, ((0, 0), (0, 125)))
    own = lax.rem(lax.axis_index("seq"), 4) * 32 + lax.broadcasted_iota(jnp.int32, (32, 128), 0)
    sel = (own == lanes()).astype(BF16)
    mixed, grad_values, grad_gates = home(outs, gates, cotangent, gate_cols, sel)
    step = 1
    while step < batch:
        sums = sums + lax.ppermute(sums, "batch", [(i, i ^ step) for i in range(batch)])
        step *= 2
    sums = sums[:, :7].T
    grad_values = grad_values.reshape(values.shape)
    return mixed, grad_values, grad_gates, grad_spectrum.transpose(0, 2, 1), sums[0:3], sums[3:6], sums[6]


def solution(mesh):
    in_specs = (
        P(None, ("batch", "seq")),
        P(None, ("batch", "seq")),
        P(None, ("batch", "seq")),
        P(),
        P(),
        P(),
        P("batch", None),
        P(),
        P("seq", None, "batch"),
    )
    out_specs = (
        P(None, ("batch", "seq")),
        P(None, ("batch", "seq")),
        P(None, ("batch", "seq")),
        P("seq", None, "batch"),
        P(None, "seq"),
        P(None, "seq"),
        P("seq"),
    )
    return jax.shard_map(per_device, mesh=mesh, in_specs=in_specs, out_specs=out_specs, check_vma=False)
```

```python
import math

import jax
import jax.numpy as jnp
import numpy as np
from jax import lax
from jax.experimental import pallas as pl
from jax.experimental.pallas import tpu as pltpu
from jax.sharding import PartitionSpec as P


BLOCK = 1024
F32, BF16 = jnp.float32, jnp.bfloat16
GRANT = 20 << 20
PARTS = 4


def cas_table():
    indices = np.arange(BLOCK, dtype=np.int32)
    products = indices[:, None] * indices[None, :] % BLOCK
    angles = products.astype(np.float32) * np.float32(2.0 * math.pi / BLOCK)
    table = (np.cos(angles) + np.sin(angles)) / np.float32(math.sqrt(BLOCK))
    return table.astype(jnp.bfloat16)


def lanes(shape=(32, 128)):
    return lax.broadcasted_iota(jnp.int32, shape, 1)


def back_in_time(now, before, steps, lane):
    return jnp.where(lane < steps, before, now)


def rolled(tile):
    return pltpu.roll(tile, 1, 1), pltpu.roll(tile, 2, 1)


def column(cols, at):
    return jnp.broadcast_to(cols[:, at : at + 1], (cols.shape[0], 128))


def gather_kernel(a_ref, b_ref, c_ref, out_ref, held, in_sems, out_sems):
    size = 32 // PARTS
    arrive, leave = [], []
    for p in range(PARTS):
        own = slice(p * size, p * size + size)
        arrive.append(
            [
                pltpu.make_async_copy(ref.at[own], held.at[own, k * 32 : k * 32 + 32, :], in_sems.at[p, k])
                for k, ref in enumerate((a_ref, b_ref, c_ref))
            ]
        )
        leave.append(pltpu.make_async_copy(held.at[own], out_ref.at[own], out_sems.at[p]))
    for part in arrive:
        for copy in part:
            copy.start()
    for part, copy in zip(arrive, leave):
        for one in part:
            one.wait()
        copy.start()
    for copy in leave:
        copy.wait()


def keep_kernel(table_ref, out_ref, sem):
    copy = pltpu.make_async_copy(table_ref, out_ref, sem)
    copy.start()
    copy.wait()


def shorten(tile, one, two, taps):
    return taps[0] * tile + taps[1] * one + taps[2] * two


def local_kernel(r_ref, cols_ref, lhs_ref):
    lane = lanes((16, 128))
    zero = jnp.zeros((16, 128), F32)
    for h in range(2):
        one, two, three = (slice(h * 16 + k * 32, h * 16 + k * 32 + 16) for k in range(3))
        cols = cols_ref[one, :]
        tv = [column(cols, k) for k in range(3)]
        tg = [column(cols, 3 + k) for k in range(3)]

        def block(i, carry):
            v1, v2, g1, g2 = carry
            rows = pl.multiple_of(i * 32, 32) + h * 16
            for t in range(8):
                piece, at = i * 4 + t // 2, slice((t % 2) * 128, (t % 2) * 128 + 128)
                v = r_ref[piece, one, at].astype(F32)
                g = r_ref[piece, two, at].astype(F32)
                c = r_ref[piece, three, at].astype(F32)
                nv1, nv2 = rolled(v)
                ng1, ng2 = rolled(g)
                short_v = shorten(v, back_in_time(nv1, v1, 1, lane), back_in_time(nv2, v2, 2, lane), tv)
                short_g = shorten(g, back_in_time(ng1, g1, 1, lane), back_in_time(ng2, g2, 2, lane), tg)
                lhs_ref[pl.ds(rows, 16), t * 128 : t * 128 + 128] = short_v.astype(BF16)
                lhs_ref[pl.ds(rows + 256, 16), t * 128 : t * 128 + 128] = (c * short_g).astype(BF16)
                v1, v2, g1, g2 = nv1, nv2, ng1, ng2
            return v1, v2, g1, g2

        lax.fori_loop(0, 8, block, (zero,) * 4)


def spread_kernel(part_ref, r_ref, rim_ref, cols_ref, tw_ref, cas_ref, out_ref, lhs):
    lane = lanes((16, 128))
    lhs[...] = part_ref[...]
    for h in range(2):
        one, two, three = (slice(h * 16 + k * 32, h * 16 + k * 32 + 16) for k in range(3))
        cols = cols_ref[one, :]
        short = []
        for k, own in enumerate((one, two)):
            tile = r_ref[0, own, 0:128].astype(F32)
            before = rolled(rim_ref[own, :].astype(F32))
            shifted = [back_in_time(a, b, n + 1, lane) for n, (a, b) in enumerate(zip(rolled(tile), before))]
            short.append(shorten(tile, *shifted, [column(cols, 3 * k + n) for n in range(3)]))
        lhs[one, 0:128] = short[0].astype(BF16)
        lhs[256 + h * 16 : 272 + h * 16, 0:128] = (r_ref[0, three, 0:128].astype(F32) * short[1]).astype(BF16)

    low = lanes((16, 128)) < 64

    def strip(n, _):
        at = pl.multiple_of(n * 256, 256)
        sums = jnp.dot(lhs[...], cas_ref[:, pl.ds(at, 256)], preferred_element_type=F32)
        for h in range(2):
            tw = tw_ref[:, pl.ds(pl.multiple_of(at + h * 128, 128), 128)]
            d = 4 * n + 2 * h
            for m in range(16):
                part = sums[m * 32 : m * 32 + 32, h * 128 : h * 128 + 128] * tw[m % 8 : m % 8 + 1, :]
                a, b = part[:16], part[16:]
                even = jnp.where(low, a, pltpu.roll(b, 64, 1))
                odd = jnp.where(low, pltpu.roll(a, 64, 1), b)
                out_ref[d, m * 16 : m * 16 + 16, :] = even.astype(BF16)
                out_ref[d + 1, m * 16 : m * 16 + 16, :] = odd.astype(BF16)
        return 0

    lax.fori_loop(0, 4, strip, 0, unroll=True)


def mix_kernel(f_ref, spec_ref, mix_ref, gs_ref, out_ref, wide_v, wide_g):
    wide = (wide_v, wide_g)
    for f in range(2):
        for b in range(16):
            wide[f][b * 128 : b * 128 + 128, :] = f_ref[b, f * 128 : f * 128 + 128, :].astype(F32)
    mixing = mix_ref[...]
    turned = mixing.T
    high = turned.astype(BF16)
    low = (turned - high.astype(F32)).astype(BF16)
    ahead = jnp.concatenate([high, low], axis=1)
    again = jnp.concatenate([jnp.concatenate([high, high], axis=1), jnp.concatenate([low, low], axis=1)], axis=0)

    for c in range(16):
        slabs = [wide[f][pl.ds(c, 128, stride=16), :].T.astype(BF16) for f in range(2)]
        both = jnp.dot(jnp.concatenate(slabs, axis=0), ahead, preferred_element_type=F32)
        both = both[:, :128] + both[:, 128:]
        sv, sg = both[:128], both[128:]
        filters = jnp.concatenate([spec_ref[c], spec_ref[16 + c]], axis=0).astype(F32)
        grad = sv * sg
        gs_ref[c] = grad[:64]
        gs_ref[16 + c] = grad[64:]
        product = jnp.concatenate([sv * filters, sg * filters], axis=0)
        top = product.astype(BF16)
        rest = (product - top.astype(F32)).astype(BF16)
        product = jnp.concatenate([top, rest], axis=1)
        sums = lax.dot_general(again, product, (((1,), (1,)), ((), ())), preferred_element_type=F32)
        sums = sums[:128] + sums[128:]
        for f in range(2):
            wide[f][pl.ds(c, 128, stride=16), :] = sums[:, f * 128 : f * 128 + 128]
    for f in range(2):
        for b in range(16):
            out_ref[b, f * 128 : f * 128 + 128, :] = wide[f][b * 128 : b * 128 + 128, :].astype(BF16)


def back_kernel(y_ref, r_ref, rim_ref, cols_ref, tw_ref, cas_ref, out_ref, head_ref, lhs):
    low = lanes((16, 128)) < 64

    def unpack(y, _):
        at = pl.multiple_of(y * 128, 128)
        tw = tw_ref[:, pl.ds(at, 128)]
        for m in range(16):
            e = y_ref[2 * y, m * 16 : m * 16 + 16, :].astype(F32)
            o = y_ref[2 * y + 1, m * 16 : m * 16 + 16, :].astype(F32)
            row = tw[m % 8 : m % 8 + 1, :]
            a = jnp.where(low, e, pltpu.roll(o, 64, 1)) * row
            b = jnp.where(low, pltpu.roll(e, 64, 1), o) * row
            lhs[m * 32 : m * 32 + 16, pl.ds(at, 128)] = a.astype(BF16)
            lhs[m * 32 + 16 : m * 32 + 32, pl.ds(at, 128)] = b.astype(BF16)
        return 0

    lax.fori_loop(0, 8, unpack, 0)

    def strip(n, _):
        at = pl.multiple_of(n * 256, 256)
        sums = jnp.dot(lhs[...], cas_ref[:, pl.ds(at, 256)], preferred_element_type=F32)
        out_ref[:, pl.ds(at, 256)] = sums.astype(BF16)
        return 0

    lax.fori_loop(0, 4, strip, 0, unroll=True)

    lane = lanes()
    cols = cols_ref[...]
    v, g, c = (r_ref[0, k * 32 : k * 32 + 32, 0:128].astype(F32) for k in range(3))
    before_v, before_g = rim_ref[0:32, :].astype(F32), rim_ref[32:64, :].astype(F32)
    short_v, short_g = v * column(cols, 0), g * column(cols, 3)
    for k in (1, 2):
        short_v += column(cols, k) * back_in_time(pltpu.roll(v, k, 1), pltpu.roll(before_v, k, 1), k, lane)
        short_g += column(cols, 3 + k) * back_in_time(pltpu.roll(g, k, 1), pltpu.roll(before_g, k, 1), k, lane)
    short_v = short_v.astype(BF16).astype(F32)
    grad_long = (c * short_g).astype(BF16).astype(F32)
    skip = column(cols, 6)
    head_ref[0:32, :] = skip * grad_long + out_ref[256:288, 0:128].astype(F32)
    head_ref[32:64, :] = c * (out_ref[0:32, 0:128].astype(F32) + skip * short_v)


def finish(r_ref, d_ref, rim_ref, cols_ref, stage, heads, sums_ref, first, count, following, on_block):
    lane = lanes((16, 128))

    def ahead(tile):
        return pltpu.roll(tile, 127, 1), pltpu.roll(tile, 126, 1)

    for h in range(2):
        one, two, three = (slice(h * 16 + k * 32, h * 16 + k * 32 + 16) for k in range(3))
        cols = cols_ref[one, :]
        tv = [column(cols, k) for k in range(3)]
        tg = [column(cols, 3 + k) for k in range(3)]
        skip = column(cols, 6)

        def gradients(v, vb, g, gb, c, long_v, back_g):
            short_v = shorten(v, *vb, tv).astype(BF16).astype(F32)
            short_g = shorten(g, *gb, tg)
            grad_long = (c * short_g).astype(BF16).astype(F32)
            direct = long_v + skip * short_v
            return short_v, short_g, grad_long, direct, skip * grad_long + back_g, c * direct

        def block(step, carry):
            i = first + count - 1 - step
            (v, v1, v2), (g, g1, g2), nv, acc = carry
            rows = pl.multiple_of(i * 32, 32) + h * 16
            for t in reversed(range(8)):
                piece, at = i * 4 + t // 2, slice((t % 2) * 128, (t % 2) * 128 + 128)
                if t > 0:
                    piece_b, at_b = i * 4 + (t - 1) // 2, slice(((t - 1) % 2) * 128, ((t - 1) % 2) * 128 + 128)
                    pv = r_ref[piece_b, one, at_b].astype(F32)
                    pg = r_ref[piece_b, two, at_b].astype(F32)
                else:
                    inside = i > 0
                    piece_b = jnp.maximum(i * 4 - 1, 0)
                    pv = jnp.where(inside, r_ref[piece_b, one, 128:256].astype(F32), rim_ref[one, :].astype(F32))
                    pg = jnp.where(inside, r_ref[piece_b, two, 128:256].astype(F32), rim_ref[two, :].astype(F32))
                pv1, pv2 = rolled(pv)
                pg1, pg2 = rolled(pg)
                vb = back_in_time(v1, pv1, 1, lane), back_in_time(v2, pv2, 2, lane)
                gb = back_in_time(g1, pg1, 1, lane), back_in_time(g2, pg2, 2, lane)
                c = r_ref[piece, three, at].astype(F32)
                long_v = d_ref[pl.ds(rows, 16), t * 128 : t * 128 + 128].astype(F32)
                back_g = d_ref[pl.ds(rows + 256, 16), t * 128 : t * 128 + 128].astype(F32)
                short_v, _, grad_long, direct, gsv, gsg = gradients(v, vb, g, gb, c, long_v, back_g)
                wv = ahead(gsv)
                put = piece - first * 4
                stage[put, one, at] = direct.astype(BF16)
                stage[put, two, at] = shorten(
                    gsv, jnp.where(lane > 126, nv[0], wv[0]), jnp.where(lane > 125, nv[1], wv[1]), tv
                ).astype(BF16)
                if t % 2 == 0:
                    heads[pl.ds(pl.multiple_of(put * 32, 32) + h * 16, 16), :] = gsg.astype(BF16)
                terms = (gsv * v, gsv * vb[0], gsv * vb[1], gsg * g, gsg * gb[0], gsg * gb[1], grad_long * short_v)
                acc = tuple(a + b for a, b in zip(acc, terms))
                v, v1, v2, g, g1, g2, nv = pv, pv1, pv2, pg, pg1, pg2, wv
            if h == 1:
                on_block(i - first)
            return (v, v1, v2), (g, g1, g2), nv, acc

        end = first * 4 + count * 4 - 1
        last_v = r_ref[end, one, 128:256].astype(F32)
        last_g = r_ref[end, two, 128:256].astype(F32)
        last_v = last_v, *rolled(last_v)
        last_g = last_g, *rolled(last_g)
        if following is None:
            rows = (first + count) * 32 + h * 16
            next_v, next_g, c = (r_ref[end + 1, own, 0:128].astype(F32) for own in (one, two, three))
            vb = [back_in_time(a, b, n + 1, lane) for n, (a, b) in enumerate(zip(rolled(next_v), last_v[1:]))]
            gb = [back_in_time(a, b, n + 1, lane) for n, (a, b) in enumerate(zip(rolled(next_g), last_g[1:]))]
            long_v = d_ref[rows : rows + 16, 0:128].astype(F32)
            back_g = d_ref[rows + 256 : rows + 272, 0:128].astype(F32)
            gsv = gradients(next_v, vb, next_g, gb, c, long_v, back_g)[4]
        else:
            gsv = following[one, :]
        zero = jnp.zeros((16, 128), F32)
        start = last_v, last_g, ahead(gsv), (zero,) * 7
        acc = lax.fori_loop(0, count, block, start)[3]
        total = zero
        for k in range(7):
            total = jnp.where(lane == k, jnp.sum(acc[k], axis=1, keepdims=True), total)
        sums_ref[one, :] = total


def most_kernel(d_ref, r_ref, rim_ref, cols_ref, out_ref, sums_ref, heads_ref, stage, sems):
    def leave(i):
        own = pl.ds(i * 4, 4)
        return pltpu.make_async_copy(stage.at[own], out_ref.at[own, 0:64, :], sems.at[i])

    def on_block(i):
        leave(i).start()

    finish(r_ref, d_ref, rim_ref, cols_ref, stage, heads_ref, sums_ref, 0, 7, None, on_block)
    for i in range(7):
        leave(i).wait()


def last_kernel(
    most_ref, d_ref, r_ref, rim_ref, next_ref, cols_ref, some_ref, heads_ref, out_ref, sums_ref, stage, edges, held, sems
):
    line = lax.broadcasted_iota(jnp.int32, (8, 128), 0)
    lane = lanes((8, 128))
    after = ((line < 2) & (lane == line)).astype(F32).astype(BF16)
    before = ((line > 1) & (line < 4) & (lane == line + 124)).astype(F32).astype(BF16)
    dims = (((1,), (1,)), ((), ()))

    def edge_rows(j, ahead):
        pieces = [r_ref[p, 32:64, 128:256] if p >= 0 else rim_ref[32:64, :] for p in range(4 * j - 1, 4 * j + 3)]
        rows = lax.dot_general(after, ahead, dims, preferred_element_type=F32)
        rows += lax.dot_general(before, jnp.concatenate(pieces, axis=0), dims, preferred_element_type=F32)
        for p in range(4 * j, 4 * j + 4):
            edges[p, :, 0:128] = rows.astype(BF16)

    edges[:, :, 128:256] = jnp.zeros((32, 8, 128), BF16)
    copies = [
        pltpu.make_async_copy(edges.at[0:24], out_ref.at[0:24, 64:72, :], sems.at[0]),
        pltpu.make_async_copy(stage, out_ref.at[28:32, 0:64, :], sems.at[1]),
        pltpu.make_async_copy(edges.at[24:32], out_ref.at[24:32, 64:72, :], sems.at[2]),
    ]
    for j in range(6):
        edge_rows(j, heads_ref[j * 128 + 32 : j * 128 + 160, :])
    copies[0].start()
    finish(r_ref, d_ref, rim_ref, cols_ref, stage, held, sums_ref, 7, 1, next_ref, lambda i: None)
    copies[1].start()
    held[128:160, :] = next_ref[32:64, :].astype(BF16)
    edge_rows(6, jnp.concatenate([heads_ref[800:896, :], held[0:32, :]], axis=0))
    edge_rows(7, held[32:160, :])
    copies[2].start()
    sums_ref[...] = sums_ref[...] + some_ref[...]
    for copy in copies:
        copy.wait()


def home_kernel(
    u_ref, g_ref, c_ref, cols_ref, sel_ref, mixed_ref, gv_ref, gg_ref, stage_m, stage_g, turned, sems
):
    direct = pltpu.make_async_copy(u_ref.at[:, 32:64, :], gv_ref, sems.at[0, 2])
    direct.start()
    lane = lanes((16, 128))
    for j in range(2):
        edge = u_ref[j * 16 : j * 16 + 16, 64:72, 0:128].astype(F32).reshape(128, 128).astype(BF16)
        turned[j] = lax.dot_general(sel_ref[...], edge, (((1,), (1,)), ((), ())), preferred_element_type=F32)

    def leave(j):
        own = pl.ds(pl.multiple_of(j * 512, 512), 512)
        return (
            pltpu.make_async_copy(stage_m.at[own], mixed_ref.at[own], sems.at[j, 0]),
            pltpu.make_async_copy(stage_g.at[own], gg_ref.at[own], sems.at[j, 1]),
        )

    def half(j, _):
        for k in range(16):
            for h in range(2):
                q = j * 16 + k
                rows = pl.ds(pl.multiple_of(q * 32, 32) + h * 16, 16)
                own = slice(h * 16, h * 16 + 16)
                after0, after1, before2, before1 = (
                    jnp.broadcast_to(turned[j, own, k * 8 + n : k * 8 + n + 1], (16, 128)) for n in range(4)
                )
                cols = cols_ref[rows, :]
                tg = [column(cols, n) for n in range(3)]
                g, c, u = (
                    [ref[:, at : at + 128].astype(F32) for at in (0, 128)]
                    for ref in (g_ref.at[rows], c_ref.at[rows], u_ref.at[q, own])
                )
                ones, twos = zip(*(rolled(x) for x in g))
                one = jnp.where(lane < 1, before1, ones[0]), back_in_time(ones[1], ones[0], 1, lane)
                two = jnp.where(lane < 1, before2, back_in_time(twos[0], before1, 2, lane)), back_in_time(twos[1], twos[0], 2, lane)
                s = [a * b for a, b in zip(c, u)]
                left = [(pltpu.roll(x, 127, 1), pltpu.roll(x, 126, 1)) for x in s]
                next1 = jnp.where(lane > 126, left[1][0], left[0][0]), jnp.where(lane > 126, after0, left[1][0])
                next2 = (
                    jnp.where(lane > 125, left[1][1], left[0][1]),
                    jnp.where(lane > 126, after1, jnp.where(lane > 125, after0, left[1][1])),
                )
                for n, at in enumerate((0, 128)):
                    stage_m[rows, at : at + 128] = (shorten(g[n], one[n], two[n], tg) * u[n]).astype(BF16)
                    stage_g[rows, at : at + 128] = shorten(s[n], next1[n], next2[n], tg).astype(BF16)
        for copy in leave(j):
            copy.start()
        return 0

    lax.fori_loop(0, 2, half, 0)
    direct.wait()
    for j in range(2):
        for copy in leave(j):
            copy.wait()


VMEM = pl.BlockSpec(memory_space=pltpu.VMEM)
ANY = pl.BlockSpec(memory_space=pl.ANY)


def call(kernel, outs, scratch, flops, moved, *args, **more):
    return pl.pallas_call(
        kernel,
        **{"in_specs": [VMEM] * len(args), "out_specs": [VMEM] * len(outs), **more},
        compiler_params=pltpu.CompilerParams(vmem_limit_bytes=GRANT),
        out_shape=[jax.ShapeDtypeStruct(s, d) for s, d in outs],
        scratch_shapes=[s if d is None else pltpu.VMEM(s, d) for s, d in scratch],
        cost_estimate=pl.CostEstimate(flops=flops, bytes_accessed=moved, transcendentals=0),
    )(*args)


def local(r, cols):
    return call(local_kernel, [((512, 1024), BF16)], [], 1 << 24, 4 << 20, r, cols)[0]


def spread(part, r, rim, cols, twiddle, cas):
    return call(
        spread_kernel,
        [((16, 256, 128), BF16)],
        [((512, 1024), BF16)],
        1 << 30,
        5 << 20,
        part,
        r,
        rim,
        cols,
        twiddle,
        cas,
    )[0]


def mix(by_freq, spectrum, mixing):
    return call(
        mix_kernel,
        [((32, 64, 128), F32), ((16, 256, 128), BF16)],
        [((2048, 128), F32), ((2048, 128), F32)],
        1 << 30,
        5 << 20,
        by_freq,
        spectrum,
        mixing,
    )


def back(returned, r, rim, cols, twiddle, cas):
    return call(
        back_kernel,
        [((512, 1024), BF16), ((64, 128), F32)],
        [((512, 1024), BF16)],
        1 << 30,
        5 << 20,
        returned,
        r,
        rim,
        cols,
        twiddle,
        cas,
    )


def most(d, r, rim, cols):
    return call(
        most_kernel,
        [((32, 72, 256), BF16), ((32, 128), F32), ((896, 128), BF16)],
        [((28, 64, 256), BF16), (pltpu.SemaphoreType.DMA((7,)), None)],
        1 << 25,
        8 << 20,
        d,
        r,
        rim,
        cols,
        out_specs=[ANY, VMEM, VMEM],
    )


def last(done, d, r, rim, following, cols, sums, heads):
    return call(
        last_kernel,
        [((32, 72, 256), BF16), ((32, 128), F32)],
        [
            ((4, 64, 256), BF16),
            ((32, 8, 256), BF16),
            ((160, 128), BF16),
            (pltpu.SemaphoreType.DMA((3,)), None),
        ],
        1 << 22,
        1 << 20,
        done,
        d,
        r,
        rim,
        following,
        cols,
        sums,
        heads,
        in_specs=[ANY] + [VMEM] * 7,
        out_specs=[ANY, VMEM],
        input_output_aliases={0: 0},
    )


def home(u, gates, cotangent, cols, sel):
    return call(
        home_kernel,
        [((1024, 256), BF16), ((32, 32, 256), BF16), ((1024, 256), BF16)],
        [
            ((1024, 256), BF16),
            ((1024, 256), BF16),
            ((2, 32, 128), F32),
            (pltpu.SemaphoreType.DMA((2, 3)), None),
        ],
        1 << 24,
        6 << 20,
        u,
        gates,
        cotangent,
        cols,
        sel,
        out_specs=[ANY] * 3,
    )


def gather(*fields):
    return pl.pallas_call(
        gather_kernel,
        in_specs=[pl.BlockSpec(memory_space=pl.ANY)] * 3,
        out_specs=pl.BlockSpec(memory_space=pl.ANY),
        out_shape=jax.ShapeDtypeStruct((32, 96, 256), BF16),
        scratch_shapes=[
            pltpu.VMEM((32, 96, 256), BF16),
            pltpu.SemaphoreType.DMA((PARTS, 3)),
            pltpu.SemaphoreType.DMA((PARTS,)),
        ],
    )(*fields)


def keep(table):
    return pl.pallas_call(
        keep_kernel,
        in_specs=[pl.BlockSpec(memory_space=pl.ANY)],
        out_specs=pl.BlockSpec(memory_space=pltpu.VMEM),
        out_shape=jax.ShapeDtypeStruct(table.shape, table.dtype),
        scratch_shapes=[pltpu.SemaphoreType.DMA(())],
        compiler_params=pltpu.CompilerParams(vmem_limit_bytes=GRANT),
        cost_estimate=pl.CostEstimate(flops=0, bytes_accessed=4 << 20, transcendentals=0),
    )(table)


def exchange(array, axis):
    return lax.all_to_all(array, axis, 0, 0, tiled=True)


def per_device(values, gates, cotangent, taps_values, taps_gates, skip_gain, twiddle, mixing, spectrum):
    batch = lax.axis_size("batch")
    raw = gather(*(x.reshape(32, 32, 256) for x in (values, gates, cotangent)))
    r = exchange(raw, "seq")
    cas = keep(jnp.asarray(cas_table()))
    gains = jnp.concatenate([taps_values, taps_gates, skip_gain[None]], axis=0)
    cols = lax.dynamic_slice(gains, (0, lax.axis_index("seq") * 32), (7, 32))
    cols = jnp.pad(cols.T, ((0, 0), (0, 121)))
    rim = lax.ppermute(r[31, :64, 128:], "batch", [(i, i + 1) for i in range(batch - 1)])
    by_freq = exchange(spread(local(r, cols), r, rim, cols, twiddle, cas), "batch")
    grad_spectrum, weighted = mix(by_freq, spectrum.transpose(0, 2, 1), mixing)
    d, head = back(exchange(weighted, "batch"), r, rim, cols, twiddle, cas)
    following = lax.ppermute(head, "batch", [(i + 1, i) for i in range(batch - 1)])
    done, sums, heads = most(d, r, rim, cols)
    done, sums = last(done, d, r, rim, following, cols, sums, heads)
    outs = exchange(done, "seq")
    gate_cols = jnp.pad(taps_gates.T, ((0, 0), (0, 125)))
    own = lax.rem(lax.axis_index("seq"), 4) * 32 + lax.broadcasted_iota(jnp.int32, (32, 128), 0)
    sel = (own == lanes()).astype(BF16)
    mixed, grad_values, grad_gates = home(outs, gates, cotangent, gate_cols, sel)
    step = 1
    while step < batch:
        sums = sums + lax.ppermute(sums, "batch", [(i, i ^ step) for i in range(batch)])
        step *= 2
    sums = sums[:, :7].T
    grad_values = grad_values.reshape(values.shape)
    return mixed, grad_values, grad_gates, grad_spectrum.transpose(0, 2, 1), sums[0:3], sums[3:6], sums[6]


def solution(mesh):
    in_specs = (
        P(None, ("batch", "seq")),
        P(None, ("batch", "seq")),
        P(None, ("batch", "seq")),
        P(),
        P(),
        P(),
        P("batch", None),
        P(),
        P("seq", None, "batch"),
    )
    out_specs = (
        P(None, ("batch", "seq")),
        P(None, ("batch", "seq")),
        P(None, ("batch", "seq")),
        P("seq", None, "batch"),
        P(None, "seq"),
        P(None, "seq"),
        P("seq"),
    )
    return jax.shard_map(per_device, mesh=mesh, in_specs=in_specs, out_specs=out_specs, check_vma=False)
```
